32 devices in a mesh: gx: 16 (over z, y, core), gy: 2 (over x).
Axes of the slice: x: 2, y: 2, z: 4, core: 2. Of those that a mesh axis runs over, the one named last changes fastest.
Arguments:
- field: float32 [6, 16, 256, 256], P(None, None, 'gx', 'gy'), may hold values from -6 to 6
- driver: float32 [6, 16, 256, 256], P(None, None, 'gx', 'gy'), may hold values from -6 to 6
- east_wind: float32 [16, 256, 256], P(None, 'gx', 'gy'), may hold values from -0.4 to 0.4
- north_wind: float32 [16, 256, 256], P(None, 'gx', 'gy'), may hold values from -0.4 to 0.4
Outputs:
- advected: float32 [6, 16, 256, 256], P(None, None, 'gx', 'gy')
- coeffs: float32 [6, 16, 4096], replicated
The draws below stay inside these ranges and needn't reach their ends.
All inputs are finite; a program needn't handle non-finite values.
Results may differ from the reference program's by a relative error of at most 0.000098.
Values sent between devices are 32-bit elements; how exact they have to be, the bound alone decides.
A program may use at most 128 MiB of HBM per device.

```python
import math
import jax
import jax.numpy as jnp
from jax import lax

TR = 6
LEV = 16
MX = 64
MY = 64
NX = 256
NY = 256


def levels(rng, extent, split, least, largest):
    factor_of, own = 1.0, jax.random.fold_in(rng, 6)
    for position, blocks in split:
        heights = jnp.exp(jax.random.uniform(jax.random.fold_in(own, position), (blocks,), jnp.float32, least / len(split), largest / len(split)))
        factor_of = factor_of * jnp.repeat(heights, extent[position] // blocks).reshape([-1 if axis == position else 1 for axis in range(len(extent))])
    return factor_of


def centred(own_key, shape, spread, reach, shards=(), kind=jnp.bfloat16):
    level = levels(own_key, shape, shards, -0.22, 0.18) if shards else 1.0
    drawn = jax.random.normal(own_key, shape, jnp.float32) * spread * level
    return jnp.minimum(jnp.maximum(drawn, -reach), reach).astype(kind)


def setup_inputs(seed: int = 0) -> dict:
    arg_keys = jax.random.split(jax.random.key(seed), 5)
    return {
        "field": centred(arg_keys[0], (TR, LEV, NX, NY), 1.0, 6.0, ((2, 16), (3, 2)), jnp.float32),
        "driver": centred(arg_keys[1], (TR, LEV, NX, NY), 1.0, 6.0, ((2, 16), (3, 2)), jnp.float32),
        "east_wind": jnp.clip(jax.random.uniform(arg_keys[2], (LEV, NX, NY), jnp.float32, -0.4, 0.4) * levels(arg_keys[2], (LEV, NX, NY), ((1, 16), (2, 2)), -0.4, 0.0), -0.4, 0.4),
        "north_wind": jnp.clip(jax.random.uniform(arg_keys[3], (LEV, NX, NY), jnp.float32, -0.4, 0.4) * levels(arg_keys[3], (LEV, NX, NY), ((1, 16), (2, 2)), -0.4, 0.0), -0.4, 0.4),
    }


def cosine_table(first, count, total, modes):
    indices = first + jnp.arange(count, dtype=jnp.int32)
    wavenum = jnp.arange(modes, dtype=jnp.int32)
    phases = (wavenum[None, :] * (2 * indices[:, None] + 1)).astype(jnp.float32)
    cosines = jnp.cos(phases * (math.pi / (2.0 * total)))
    weight = jnp.where(wavenum == 0, math.sqrt(1.0 / total), math.sqrt(2.0 / total)).astype(jnp.float32)
    return cosines * weight[None, :]

def upwind(tracer, winds):
    east = winds[0]
    north = winds[1]
    east_flux = jnp.maximum(east[:, :-1, :], 0.0) * tracer[..., :-1, :] + jnp.minimum(east[:, :-1, :], 0.0) * tracer[..., 1:, :]
    north_flux = jnp.maximum(north[:, :, :-1], 0.0) * tracer[..., :, :-1] + jnp.minimum(north[:, :, :-1], 0.0) * tracer[..., :, 1:]
    inner = tracer[..., 1:-1, 1:-1]
    inner = inner - (east_flux[..., 1:, 1:-1] - east_flux[..., :-1, 1:-1])
    return inner - (north_flux[..., 1:-1, 1:] - north_flux[..., 1:-1, :-1])

def reference(field, driver, east_wind, north_wind):
    high = lax.Precision.HIGHEST
    x_table = cosine_table(0, NX, NX, MX)
    y_table = cosine_table(0, NY, NY, MY)
    departure = driver - field
    half_proj = jnp.einsum('tlxy,xm->tlmy', departure, x_table, precision=high)
    modal = jnp.einsum('tlmy,yn->tlmn', half_proj, y_table, precision=high)
    large_scale = jnp.einsum('tlmn,yn->tlmy', modal, y_table, precision=high)
    large_scale = jnp.einsum('tlmy,xm->tlxy', large_scale, x_table, precision=high)
    nudged = field + 0.5 * large_scale
    xpos = jnp.arange(NX, dtype=jnp.int32)
    ypos = jnp.arange(NY, dtype=jnp.int32)
    east_face = jnp.where(xpos[None, :, None] == NX - 1, jnp.float32(0.0), east_wind)
    north_face = jnp.where(ypos[None, None, :] == NY - 1, jnp.float32(0.0), north_wind)
    winds = jnp.pad(jnp.stack([east_face, north_face]), ((0, 0), (0, 0), (1, 1), (1, 1)))
    current = nudged
    for sweep in range(2):
        current = upwind(jnp.pad(current, ((0, 0), (0, 0), (1, 1), (1, 1))), winds)
    coeffs = modal.reshape(TR, LEV, MX * MY)
    return (current, coeffs)
```

```python
import math

import jax
import jax.numpy as jnp
import ml_dtypes
import numpy as np
from jax import lax
from jax.experimental import pallas as pl
from jax.experimental.pallas import tpu as pltpu
from jax.sharding import PartitionSpec as P

MX = 64
MY = 64
MESH = pl.DeviceIdType.MESH


def shifted(value, axis, steps):
    count = lax.axis_size(axis)
    first, last = (max(0, -steps), min(count, count - steps))
    return lax.ppermute(value, axis, [(source, source + steps) for source in range(first, last)])


def padded(x, sides, width):
    for axis, dim in sides:
        peers, length = (lax.axis_size(axis), x.shape[dim])
        up = [(i, (i + 1) % peers) for i in range(peers - 1)]
        down = [(j, i) for i, j in up]
        last = lax.slice_in_dim(x, length - width, length, axis=dim)
        first = lax.slice_in_dim(x, 0, width, axis=dim)
        before = lax.ppermute(last, axis, up)
        after = lax.ppermute(first, axis, down)
        x = jnp.concatenate([before, x, after], axis=dim)
    return x


def cosine_table(first, count, total, modes):
    indices = first + jnp.arange(count, dtype=jnp.int32)
    wavenum = jnp.arange(modes, dtype=jnp.int32)
    phases = (wavenum[None, :] * (2 * indices[:, None] + 1)).astype(jnp.float32)
    cosines = jnp.cos(phases * (math.pi / (2.0 * total)))
    weight = jnp.where(wavenum == 0, math.sqrt(1.0 / total), math.sqrt(2.0 / total)).astype(
        jnp.float32
    )
    return cosines * weight[None, :]


def upwind(tracer, winds):
    east = winds[0]
    north = winds[1]
    east_flux = (
        jnp.maximum(east[:, :-1, :], 0.0) * tracer[..., :-1, :]
        + jnp.minimum(east[:, :-1, :], 0.0) * tracer[..., 1:, :]
    )
    north_flux = (
        jnp.maximum(north[:, :, :-1], 0.0) * tracer[..., :, :-1]
        + jnp.minimum(north[:, :, :-1], 0.0) * tracer[..., :, 1:]
    )
    inner = tracer[..., 1:-1, 1:-1]
    inner = inner - (east_flux[..., 1:, 1:-1] - east_flux[..., :-1, 1:-1])
    return inner - (north_flux[..., 1:-1, 1:] - north_flux[..., 1:-1, :-1])


def shards(field, driver, east_wind, north_wind):
    high = lax.Precision.HIGHEST
    tracers, levels, strip_cols, band_rows = field.shape
    nx_total = strip_cols * lax.axis_size("gx")
    ny_total = band_rows * lax.axis_size("gy")
    x_first = lax.axis_index("gx") * strip_cols
    y_first = lax.axis_index("gy") * band_rows
    x_table = cosine_table(x_first, strip_cols, nx_total, MX)
    y_table = cosine_table(y_first, band_rows, ny_total, MY)
    departure = driver - field
    half_proj = jnp.einsum("tlxy,xm->tlmy", departure, x_table, precision=high)
    partial_modes = jnp.einsum("tlmy,yn->tlmn", half_proj, y_table, precision=high)
    partial_modes = partial_modes.reshape(tracers, levels, MX * MY)
    coeffs = lax.psum(partial_modes, ("gx", "gy"))
    modal = coeffs.reshape(tracers, levels, MX, MY)
    large_scale = jnp.einsum("tlmn,yn->tlmy", modal, y_table, precision=high)
    large_scale = jnp.einsum("tlmy,xm->tlxy", large_scale, x_table, precision=high)
    nudged = field + 0.5 * large_scale
    xpos = x_first + jnp.arange(strip_cols, dtype=jnp.int32)
    ypos = y_first + jnp.arange(band_rows, dtype=jnp.int32)
    east_face = jnp.where(xpos[None, :, None] == nx_total - 1, jnp.float32(0.0), east_wind)
    north_face = jnp.where(ypos[None, None, :] == ny_total - 1, jnp.float32(0.0), north_wind)
    east_below = shifted(east_face[:, -1:, :], "gx", 1)
    north_below = shifted(north_face[:, :, -1:], "gy", 1)
    east_ext = jnp.concatenate([east_below, east_face, jnp.zeros_like(east_below)], axis=1)
    east_ext = jnp.pad(east_ext, ((0, 0), (0, 0), (1, 1)))
    north_ext = jnp.concatenate([north_below, north_face, jnp.zeros_like(north_below)], axis=2)
    north_ext = jnp.pad(north_ext, ((0, 0), (1, 1), (0, 0)))
    wind_ext = jnp.stack([east_ext, north_ext])
    advected = nudged
    for sweep in range(2):
        field_ext = padded(advected, (("gx", 2), ("gy", 3)), 1)
        advected = upwind(field_ext, wind_ext)
    return (advected, coeffs)


def split(value):
    high = value.astype(jnp.bfloat16)
    return high, (value - high.astype(jnp.float32)).astype(jnp.bfloat16)


def split_table(table):
    table = np.asarray(table, np.float32)
    high = table.astype(ml_dtypes.bfloat16)
    low = (table - high.astype(np.float32)).astype(ml_dtypes.bfloat16)
    return high, low


def table64(total, modes):
    index = np.arange(total)[:, None]
    wave = np.arange(modes)[None, :]
    weight = np.where(wave == 0, math.sqrt(1.0 / total), math.sqrt(2.0 / total))
    turns = (wave * (2 * index + 1)) % (4 * total)
    return np.cos(turns * (math.pi / (2.0 * total))) * weight


def dot(a, b):
    return jnp.dot(a, b, preferred_element_type=jnp.float32)


def tables(gxn, gyn, strip, band):
    bx = table64(gxn * strip, MX)
    by = table64(gyn * band, MY)
    half = strip // 2
    forward_y = np.zeros((gyn, 2 * band, 2 * MY))
    for g in range(gyn):
        own = by[g * band : (g + 1) * band]
        forward_y[g, :band, :MY] = own
        forward_y[g, band:, MY:] = own
    wy = np.stack(split_table(forward_y), axis=1)
    bx4 = bx.reshape(gxn, 2, half, MX // 2, 2)
    forward_x = np.broadcast_to(
        bx4.transpose(1, 4, 3, 0, 2)[:, :, :, :, None, :], (2, 2, MX // 2, gxn, gyn, half)
    )
    wx = np.stack(split_table(forward_x.reshape(2 * MX, gxn * gyn * half)))
    inverse_x = np.zeros((gxn, 2, strip + 8, MX // 2))
    for g in range(gxn):
        for row in range(strip + 8):
            if row < strip + 2:
                x = g * strip + row
            elif row >= strip + 6:
                x = g * strip + row - strip - 8
            else:
                continue
            if 0 <= x < gxn * strip:
                inverse_x[g, :, row] = bx[x].reshape(MX // 2, 2).T
    high, low = split_table(inverse_x.reshape(gxn, 2 * (strip + 8), MX // 2))
    xb = np.concatenate([high, high, low], axis=2)
    inverse_y = np.zeros((gyn, 2 * MY, gyn * band))
    for g in range(gyn):
        rolled = 0.5 * np.roll(by, -g * band, axis=0).T
        inverse_y[g, :MY] = rolled
        inverse_y[g, MY:] = rolled
    wi = np.stack(split_table(inverse_y), axis=1)
    return wy, wx, xb, wi


def gather_kernel(
    field, driver, east, north, wy, wx, coef, halo, ytile,
    part, recv, edge, ysend, wind,
    a2a_s, a2a_r, halo_s, halo_r, y_s, y_r, z_s, z_r, p2_s, p2_r, p3_s, p3_r, core_s, core_r,
):
    gx = lax.axis_index("gx")
    gy = lax.axis_index("gy")
    gxn, gyn = lax.axis_size("gx"), lax.axis_size("gy")
    count = gxn * gyn
    me = gx * gyn + gy
    fields, strip, band = field.shape
    levels = east.shape[0]
    own = fields // count

    barrier = pltpu.get_barrier_semaphore()

    def greet(rel, carry):
        d = (me + rel) % count
        pl.semaphore_signal(
            barrier, inc=1, device_id=(d // gyn, d % gyn), device_id_type=MESH
        )
        return carry

    lax.fori_loop(1, count, greet, 0)

    wh, wl = wy[gy, 0], wy[gy, 1]
    chunk = 4 * own
    for c in range(fields // chunk):
        rows = pl.ds(c * chunk, chunk)
        departure = driver[rows] - field[rows]
        lhs = jnp.concatenate([departure[:, : strip // 2], departure[:, strip // 2 :]], axis=2)
        high, low = split(lhs.reshape(chunk * strip // 2, 2 * band))
        got = dot(high, wh) + (dot(low, wh) + dot(high, wl))
        part[pl.ds(c * 4, 4)] = got.reshape(4, own, strip // 2, 2 * MY)
    pl.semaphore_wait(barrier, count - 1)

    def exchange(d, s):
        return pltpu.make_async_remote_copy(
            src_ref=part.at[d], dst_ref=recv.at[s], send_sem=a2a_s.at[d], recv_sem=a2a_r.at[s],
            device_id=(d // gyn, d % gyn), device_id_type=MESH,
        )

    def send(rel, carry):
        exchange((me + rel) % count, me).start()
        return carry

    lax.fori_loop(1, count, send, 0)
    recv[me] = part[me]

    row = lax.broadcasted_iota(jnp.int32, (levels, strip, band), 1) + gx * strip
    wind[pl.ds(0, levels)] = jnp.where(row == gxn * strip - 1, 0.0, east[...])
    col = lax.broadcasted_iota(jnp.int32, (levels, strip, band), 2) + gy * band
    wind[pl.ds(levels, levels)] = jnp.where(col == gyn * band - 1, 0.0, north[...])

    for side in range(2):
        for k in range(2):
            r = (strip - 2 if side == 0 else 0) + k
            edge[side, k, pl.ds(0, fields)] = field[:, r, :]
            edge[side, k, pl.ds(fields, 2 * levels)] = wind[:, r, :]

    def halo_copy(side, dy):
        peer = gx + 1 if side == 0 else gx - 1
        return pltpu.make_async_remote_copy(
            src_ref=edge.at[side], dst_ref=halo.at[side, dy],
            send_sem=halo_s.at[side, dy], recv_sem=halo_r.at[side, dy],
            device_id=(peer, (gy + dy) % gyn), device_id_type=MESH,
        )

    for dy in range(2):

        @pl.when(gx < gxn - 1)
        def _():
            halo_copy(0, dy).start()

        @pl.when(gx > 0)
        def _():
            halo_copy(1, dy).start()

        @pl.when(gx == 0)
        def _():
            halo[0, dy] = jnp.zeros(halo.shape[2:], jnp.float32)

        @pl.when(gx == gxn - 1)
        def _():
            halo[1, dy] = jnp.zeros(halo.shape[2:], jnp.float32)

    for b in range((fields + 2 * levels) // 8):
        if b * 8 < fields:
            block = field[pl.ds(b * 8, 8)]
        else:
            block = wind[pl.ds(b * 8 - fields, 8)]
        turned = block.reshape(8 * strip, band).T
        ysend[b] = jnp.where(gy == 0, turned[band - 8 :], turned[:8])
    ycopy = pltpu.make_async_remote_copy(
        src_ref=ysend, dst_ref=ytile, send_sem=y_s, recv_sem=y_r,
        device_id=(gx, 1 - gy), device_id_type=MESH,
    )
    ycopy.start()

    def receive(rel, carry):
        exchange((me + rel) % count, (me + rel) % count).wait_recv()
        return carry

    lax.fori_loop(1, count, receive, 0)
    rhs = jnp.concatenate(
        [recv[:, j].reshape(count * strip // 2, 2 * MY) for j in range(own)], axis=1
    )
    high, low = split(rhs)
    modes = dot(wx[0], high) + (dot(wx[0], low) + dot(wx[1], high))
    z, y, c, x = gx // 4, (gx // 2) % 2, gx % 2, gy
    hm = MX // 2
    lane = lax.broadcasted_iota(jnp.int32, (hm, 2 * MY), 1)
    for j in range(own):
        q = modes[:, j * 2 * MY : (j + 1) * 2 * MY]
        even = q[:hm] + pltpu.roll(q[2 * hm : 3 * hm], MY, 1)
        odd = pltpu.roll(q[hm : 2 * hm], MY, 1) + q[3 * hm :]
        coef[z, y, c, x, pl.ds(j * hm, hm)] = jnp.where(lane < MY, even, odd)

    part_rows = own * hm // 2
    first, second = pl.ds(0, part_rows), pl.ds(part_rows, part_rows)
    zs = [(z + k) % 4 for k in range(4)]

    def z_copy(k, slot):
        there = coef.at[slot, y, c, x]
        return pltpu.make_async_remote_copy(
            src_ref=there, dst_ref=there, send_sem=z_s.at[k], recv_sem=z_r.at[slot],
            device_id=(zs[k] * 4 + y * 2 + c, gy), device_id_type=MESH,
        )

    def to_x(ref, s, r):
        return pltpu.make_async_remote_copy(
            src_ref=ref, dst_ref=ref, send_sem=s, recv_sem=r,
            device_id=(gx, 1 - gy), device_id_type=MESH,
        )

    def to_y(ref, s, r):
        return pltpu.make_async_remote_copy(
            src_ref=ref, dst_ref=ref, send_sem=s, recv_sem=r,
            device_id=(z * 4 + (1 - y) * 2 + c, gy), device_id_type=MESH,
        )

    def to_core(ref, s, r):
        return pltpu.make_async_remote_copy(
            src_ref=ref, dst_ref=ref, send_sem=s, recv_sem=r,
            device_id=(z * 4 + y * 2 + 1 - c, gy), device_id_type=MESH,
        )

    def second_a(k, xx):
        return to_x(coef.at[zs[k], y, c, xx, first], p2_s.at[0, k], p2_r.at[0, zs[k]])

    def second_b(k, yy):
        return to_y(coef.at[zs[k], yy, c, x, second], p2_s.at[1, k], p2_r.at[1, zs[k]])

    def third_a(k, yy):
        return to_y(coef.at[zs[k], yy, c, :, first], p3_s.at[0, k], p3_r.at[0, zs[k]])

    def third_b(k, xx):
        return to_x(coef.at[zs[k], :, c, xx, second], p3_s.at[1, k], p3_r.at[1, zs[k]])

    def core_copy(k, cc):
        return to_core(coef.at[zs[k], :, cc], core_s.at[k], core_r.at[zs[k]])

    for k in range(1, 4):
        z_copy(k, z).start()
    for k in range(4):
        if k:
            z_copy(k, zs[k]).wait_recv()
        second_a(k, x).start()
        second_b(k, y).start()
    for k in range(4):
        second_a(k, 1 - x).wait_recv()
        second_b(k, 1 - y).wait_recv()
        third_a(k, y).start()
        third_b(k, x).start()
    for k in range(4):
        third_a(k, 1 - y).wait_recv()
        third_b(k, 1 - x).wait_recv()
        core_copy(k, c).start()
    for k in range(4):
        core_copy(k, 1 - c).wait_recv()

    for k in range(1, 4):
        z_copy(k, z).wait_send()
    for k in range(4):
        second_a(k, x).wait_send()
        second_b(k, y).wait_send()
        third_a(k, y).wait_send()
        third_b(k, x).wait_send()
        core_copy(k, c).wait_send()

    def drain(rel, carry):
        exchange((me + rel) % count, me).wait_send()
        return carry

    lax.fori_loop(1, count, drain, 0)
    ycopy.wait()
    for dy in range(2):

        @pl.when(gx < gxn - 1)
        def _():
            halo_copy(0, dy).wait_send()
            halo_copy(1, dy).wait_recv()

        @pl.when(gx > 0)
        def _():
            halo_copy(1, dy).wait_send()
            halo_copy(0, dy).wait_recv()


def advect_kernel(
    field, east, north, coef, halo, ytile, xb, wi, out, coef_out, side, other, large
):
    gx = lax.axis_index("gx")
    gy = lax.axis_index("gy")
    gxn, gyn = lax.axis_size("gx"), lax.axis_size("gy")
    fields, strip, band = field.shape
    levels = east.shape[0]
    tracers = fields // levels
    ext = strip + 8
    hm = MX // 2
    total = fields + 2 * levels
    for j in range(hm):
        coef_out[:, pl.ds(j * 2 * MY, 2 * MY)] = coef[pl.ds(j, fields, stride=hm), :]
    side[...] = jnp.zeros(side.shape, jnp.float32)
    for d in range(2):
        for k in range(2):
            side[d, pl.ds(k, total, stride=8), :] = halo[1, d, k]
            side[d, pl.ds(6 + k, total, stride=8), :] = halo[0, d, k]
    gap = jnp.zeros((band - 16, 8 * strip), jnp.float32)
    for b in range(total // 8):
        tile = ytile[b]
        spread = jnp.concatenate(
            [jnp.where(gy == 0, tile, 0.0), gap, jnp.where(gy == 1, tile, 0.0)], axis=0
        )
        other[pl.ds(b * 8, 8)] = spread.T.reshape(8, strip, band)

    table = xb[gx]
    wh, wl = wi[gy, 0], wi[gy, 1]
    lane = lax.broadcasted_iota(jnp.int32, (ext, 2 * MY), 1)
    group = 4

    def inverse(g, carry):
        stack = []
        for h in range(group // 2):
            f = g * group + 2 * h
            two = jnp.concatenate(
                [
                    coef[pl.ds(pl.multiple_of(f * hm, hm), hm), :],
                    coef[pl.ds(pl.multiple_of(f * hm + hm, hm), hm), :],
                ],
                axis=1,
            )
            high, low = split(two)
            mixed = dot(table, jnp.concatenate([high, low, high], axis=0))
            for i in range(2):
                one = mixed[:, i * 2 * MY : (i + 1) * 2 * MY]
                stack.append(jnp.where(lane < MY, one[:ext], one[ext:]))
        high, low = split(jnp.concatenate(stack, axis=0))
        got = dot(high, wh) + (dot(low, wh) + dot(high, wl))
        large[pl.ds(g * group, group)] = got.reshape(group, ext, gyn * band)
        return carry

    lax.fori_loop(0, fields // group, inverse, 0, unroll=2)

    xpos = lax.broadcasted_iota(jnp.int32, (strip, band), 0) + gx * strip
    ypos = lax.broadcasted_iota(jnp.int32, (strip, band), 1) + gy * band

    def extend(own, f):
        rows = pl.ds(pl.multiple_of(f * 8, 8), 8)
        edge = jnp.concatenate([side[0, rows, :], side[1, rows, :]], axis=1)
        return jnp.concatenate([jnp.concatenate([own, other[f]], axis=1), edge], axis=0)

    def level(lev, carry):
        east_own = jnp.where(xpos == gxn * strip - 1, 0.0, east[lev])
        north_own = jnp.where(ypos == gyn * band - 1, 0.0, north[lev])
        u = extend(east_own, fields + lev)
        v = extend(north_own, fields + levels + lev)
        up, un = jnp.maximum(u, 0.0), jnp.minimum(u, 0.0)
        vp, vn = jnp.maximum(v, 0.0), jnp.minimum(v, 0.0)

        def tracer(t, inner):
            f = t * levels + lev
            q = extend(field[f], f) + large[f]
            for _ in range(2):
                flux = up * q + un * pltpu.roll(q, ext - 1, 0)
                cross = vp * q + vn * pltpu.roll(q, gyn * band - 1, 1)
                q = q - (flux - pltpu.roll(flux, 1, 0))
                q = q - (cross - pltpu.roll(cross, 1, 1))
            out[f] = q[:strip, :band]
            return inner

        lax.fori_loop(0, tracers, tracer, 0, unroll=2)
        return carry

    lax.fori_loop(0, levels, level, 0)


def fused(field, driver, east, north):
    tracers, levels, strip, band = field.shape
    gxn, gyn = lax.axis_size("gx"), lax.axis_size("gy")
    count = gxn * gyn
    fields = tracers * levels
    own = fields // count
    total = fields + 2 * levels
    wy, wx, xb, wi = tables(gxn, gyn, strip, band)
    flat = field.reshape(fields, strip, band)
    dma = pltpu.SemaphoreType.DMA
    vmem = pl.BlockSpec(memory_space=pltpu.VMEM)
    f32 = jnp.float32
    coef, halo, ytile = pl.pallas_call(
        gather_kernel,
        out_shape=(
            jax.ShapeDtypeStruct((4, 2, 2, 2, own * MX // 2, 2 * MY), f32),
            jax.ShapeDtypeStruct((2, 2, 2, total, band), f32),
            jax.ShapeDtypeStruct((total // 8, 8, 8 * strip), f32),
        ),
        in_specs=[vmem] * 6,
        out_specs=(vmem, vmem, vmem),
        scratch_shapes=[
            pltpu.VMEM((count, own, strip // 2, 2 * MY), f32),
            pltpu.VMEM((count, own, strip // 2, 2 * MY), f32),
            pltpu.VMEM((2, 2, total, band), f32),
            pltpu.VMEM((total // 8, 8, 8 * strip), f32),
            pltpu.VMEM((2 * levels, strip, band), f32),
            dma((count,)), dma((count,)), dma((2, 2)), dma((2, 2)), dma, dma,
            dma((4,)), dma((4,)), dma((2, 4)), dma((2, 4)), dma((2, 4)), dma((2, 4)),
            dma((4,)), dma((4,)),
        ],
        compiler_params=pltpu.CompilerParams(
            collective_id=0, has_side_effects=True, vmem_limit_bytes=40 << 20
        ),
        name="spectral_gather",
    )(flat, driver.reshape(fields, strip, band), east, north, jnp.asarray(wy), jnp.asarray(wx))
    advected, coeffs = pl.pallas_call(
        advect_kernel,
        out_shape=(
            jax.ShapeDtypeStruct((fields, strip, band), f32),
            jax.ShapeDtypeStruct((fields, MX * MY), f32),
        ),
        in_specs=[vmem] * 8,
        out_specs=(vmem, vmem),
        scratch_shapes=[
            pltpu.VMEM((gyn, total * 8, band), f32),
            pltpu.VMEM((total, strip, band), f32),
            pltpu.VMEM((fields, strip + 8, gyn * band), f32),
        ],
        compiler_params=pltpu.CompilerParams(vmem_limit_bytes=40 << 20),
        name="advect",
    )(
        flat, east, north, coef.reshape(fields * MX // 2, 2 * MY), halo, ytile,
        jnp.asarray(xb), jnp.asarray(wi),
    )
    return (
        advected.reshape(tracers, levels, strip, band),
        coeffs.reshape(tracers, levels, MX * MY),
    )


def body(field, driver, east, north):
    tracers, levels, strip, band = field.shape
    sizes = (lax.axis_size("gx"), lax.axis_size("gy"))
    if sizes == (16, 2) and (tracers * levels, levels, strip, band) == (96, 16, 16, 128):
        return fused(field, driver, east, north)
    return shards(field, driver, east, north)


def solution(mesh):
    placed = (
        P(None, None, "gx", "gy"),
        P(None, None, "gx", "gy"),
        P(None, "gx", "gy"),
        P(None, "gx", "gy"),
    )
    return jax.shard_map(
        body,
        mesh=mesh,
        in_specs=placed,
        out_specs=(P(None, None, "gx", "gy"), P()),
        check_vma=False,
    )
```

```python
import math

import jax
import jax.numpy as jnp
import ml_dtypes
import numpy as np
from jax import lax
from jax.experimental import pallas as pl
from jax.experimental.pallas import tpu as pltpu
from jax.sharding import PartitionSpec as P

MX = 64
MY = 64
MESH = pl.DeviceIdType.MESH


def shifted(value, axis, steps):
    count = lax.axis_size(axis)
    first, last = (max(0, -steps), min(count, count - steps))
    return lax.ppermute(value, axis, [(source, source + steps) for source in range(first, last)])


def padded(x, sides, width):
    for axis, dim in sides:
        peers, length = (lax.axis_size(axis), x.shape[dim])
        up = [(i, (i + 1) % peers) for i in range(peers - 1)]
        down = [(j, i) for i, j in up]
        last = lax.slice_in_dim(x, length - width, length, axis=dim)
        first = lax.slice_in_dim(x, 0, width, axis=dim)
        before = lax.ppermute(last, axis, up)
        after = lax.ppermute(first, axis, down)
        x = jnp.concatenate([before, x, after], axis=dim)
    return x


def cosine_table(first, count, total, modes):
    indices = first + jnp.arange(count, dtype=jnp.int32)
    wavenum = jnp.arange(modes, dtype=jnp.int32)
    phases = (wavenum[None, :] * (2 * indices[:, None] + 1)).astype(jnp.float32)
    cosines = jnp.cos(phases * (math.pi / (2.0 * total)))
    weight = jnp.where(wavenum == 0, math.sqrt(1.0 / total), math.sqrt(2.0 / total)).astype(
        jnp.float32
    )
    return cosines * weight[None, :]


def upwind(tracer, winds):
    east = winds[0]
    north = winds[1]
    east_flux = (
        jnp.maximum(east[:, :-1, :], 0.0) * tracer[..., :-1, :]
        + jnp.minimum(east[:, :-1, :], 0.0) * tracer[..., 1:, :]
    )
    north_flux = (
        jnp.maximum(north[:, :, :-1], 0.0) * tracer[..., :, :-1]
        + jnp.minimum(north[:, :, :-1], 0.0) * tracer[..., :, 1:]
    )
    inner = tracer[..., 1:-1, 1:-1]
    inner = inner - (east_flux[..., 1:, 1:-1] - east_flux[..., :-1, 1:-1])
    return inner - (north_flux[..., 1:-1, 1:] - north_flux[..., 1:-1, :-1])


def shards(field, driver, east_wind, north_wind):
    high = lax.Precision.HIGHEST
    tracers, levels, strip_cols, band_rows = field.shape
    nx_total = strip_cols * lax.axis_size("gx")
    ny_total = band_rows * lax.axis_size("gy")
    x_first = lax.axis_index("gx") * strip_cols
    y_first = lax.axis_index("gy") * band_rows
    x_table = cosine_table(x_first, strip_cols, nx_total, MX)
    y_table = cosine_table(y_first, band_rows, ny_total, MY)
    departure = driver - field
    half_proj = jnp.einsum("tlxy,xm->tlmy", departure, x_table, precision=high)
    partial_modes = jnp.einsum("tlmy,yn->tlmn", half_proj, y_table, precision=high)
    partial_modes = partial_modes.reshape(tracers, levels, MX * MY)
    coeffs = lax.psum(partial_modes, ("gx", "gy"))
    modal = coeffs.reshape(tracers, levels, MX, MY)
    large_scale = jnp.einsum("tlmn,yn->tlmy", modal, y_table, precision=high)
    large_scale = jnp.einsum("tlmy,xm->tlxy", large_scale, x_table, precision=high)
    nudged = field + 0.5 * large_scale
    xpos = x_first + jnp.arange(strip_cols, dtype=jnp.int32)
    ypos = y_first + jnp.arange(band_rows, dtype=jnp.int32)
    east_face = jnp.where(xpos[None, :, None] == nx_total - 1, jnp.float32(0.0), east_wind)
    north_face = jnp.where(ypos[None, None, :] == ny_total - 1, jnp.float32(0.0), north_wind)
    east_below = shifted(east_face[:, -1:, :], "gx", 1)
    north_below = shifted(north_face[:, :, -1:], "gy", 1)
    east_ext = jnp.concatenate([east_below, east_face, jnp.zeros_like(east_below)], axis=1)
    east_ext = jnp.pad(east_ext, ((0, 0), (0, 0), (1, 1)))
    north_ext = jnp.concatenate([north_below, north_face, jnp.zeros_like(north_below)], axis=2)
    north_ext = jnp.pad(north_ext, ((0, 0), (1, 1), (0, 0)))
    wind_ext = jnp.stack([east_ext, north_ext])
    advected = nudged
    for sweep in range(2):
        field_ext = padded(advected, (("gx", 2), ("gy", 3)), 1)
        advected = upwind(field_ext, wind_ext)
    return (advected, coeffs)


def split(value):
    high = value.astype(jnp.bfloat16)
    return high, (value - high.astype(jnp.float32)).astype(jnp.bfloat16)


def split_table(table):
    table = np.asarray(table, np.float32)
    high = table.astype(ml_dtypes.bfloat16)
    low = (table - high.astype(np.float32)).astype(ml_dtypes.bfloat16)
    return high, low


def table64(total, modes):
    index = np.arange(total)[:, None]
    wave = np.arange(modes)[None, :]
    weight = np.where(wave == 0, math.sqrt(1.0 / total), math.sqrt(2.0 / total))
    turns = (wave * (2 * index + 1)) % (4 * total)
    return np.cos(turns * (math.pi / (2.0 * total))) * weight


def dot(a, b):
    return jnp.dot(a, b, preferred_element_type=jnp.float32)


def tables(gxn, gyn, strip, band):
    bx = table64(gxn * strip, MX)
    by = table64(gyn * band, MY)
    half = strip // 2
    forward_y = np.zeros((gyn, 2 * band, 2 * MY))
    for g in range(gyn):
        own = by[g * band : (g + 1) * band]
        forward_y[g, :band, :MY] = own
        forward_y[g, band:, MY:] = own
    wy = np.stack(split_table(forward_y), axis=1)
    bx4 = bx.reshape(gxn, 2, half, MX // 2, 2)
    forward_x = np.broadcast_to(
        bx4.transpose(1, 4, 3, 0, 2)[:, :, :, :, None, :], (2, 2, MX // 2, gxn, gyn, half)
    )
    wx = np.stack(split_table(forward_x.reshape(2 * MX, gxn * gyn * half)))
    inverse_x = np.zeros((gxn, 2, strip + 8, MX // 2))
    for g in range(gxn):
        for row in range(strip + 8):
            if row < strip + 2:
                x = g * strip + row
            elif row >= strip + 6:
                x = g * strip + row - strip - 8
            else:
                continue
            if 0 <= x < gxn * strip:
                inverse_x[g, :, row] = bx[x].reshape(MX // 2, 2).T
    high, low = split_table(inverse_x.reshape(gxn, 2 * (strip + 8), MX // 2))
    xb = np.concatenate([high, high, low], axis=2)
    inverse_y = np.zeros((gyn, 2 * MY, gyn * band))
    for g in range(gyn):
        rolled = 0.5 * np.roll(by, -g * band, axis=0).T
        inverse_y[g, :MY] = rolled
        inverse_y[g, MY:] = rolled
    wi = np.stack(split_table(inverse_y), axis=1)
    return wy, wx, xb, wi


def spectral_kernel(
    field_in, driver_in, east_in, north_in, wy_in, wx_in, xb_in, wi_in, coef_out, advected,
    coef, out, packed, flat, stores, field, driver, east, north, wy, wx, xb, wi,
    part, recv, edge, ysend, wind, halo, ytile, full, winds, large, loads,
    a2a_s, a2a_r, halo_s, halo_r, y_s, y_r, z_s, z_r, p2_s, p2_r, p3_s, p3_r, core_s, core_r,
):
    gx = lax.axis_index("gx")
    gy = lax.axis_index("gy")
    gxn, gyn = lax.axis_size("gx"), lax.axis_size("gy")
    count = gxn * gyn
    me = gx * gyn + gy
    fields, strip, band = field.shape
    levels = east.shape[0]
    own = fields // count
    ext = strip + 8
    total = fields + 2 * levels
    chunk = 4 * own
    chunks = fields // chunk

    def load(src, dst, index):
        return pltpu.make_async_copy(src, dst, loads.at[index])

    def piece(src, dst, c, index):
        rows = pl.ds(c * chunk, chunk)
        return load(src.at[rows], dst.at[rows], index)

    y_table = load(wy_in.at[gy], wy, 0)
    x_table = load(wx_in, wx, 1)
    small = [
        load(east_in, east, 2),
        load(north_in, north, 3),
        load(xb_in.at[gx], xb, 4),
        load(wi_in.at[gy], wi, 5),
    ]
    pieces = [
        (piece(field_in, field, c, 6 + c), piece(driver_in, driver, c, 6 + chunks + c))
        for c in range(chunks)
    ]
    y_table.start()
    for a, b in pieces:
        a.start()
        b.start()
    x_table.start()
    for copy in small:
        copy.start()

    barrier = pltpu.get_barrier_semaphore()

    def greet(rel, carry):
        d = (me + rel) % count
        pl.semaphore_signal(
            barrier, inc=1, device_id=(d // gyn, d % gyn), device_id_type=MESH
        )
        return carry

    lax.fori_loop(1, count, greet, 0)

    y_table.wait()
    wh, wl = wy[0], wy[1]
    for c in range(chunks):
        pieces[c][0].wait()
        pieces[c][1].wait()
        rows = pl.ds(c * chunk, chunk)
        departure = driver[rows] - field[rows]
        lhs = jnp.concatenate([departure[:, : strip // 2], departure[:, strip // 2 :]], axis=2)
        high, low = split(lhs.reshape(chunk * strip // 2, 2 * band))
        got = dot(high, wh) + (dot(low, wh) + dot(high, wl))
        part[pl.ds(c * 4, 4)] = got.reshape(4, own, strip // 2, 2 * MY)
    pl.semaphore_wait(barrier, count - 1)

    def exchange(d, s):
        return pltpu.make_async_remote_copy(
            src_ref=part.at[d], dst_ref=recv.at[s], send_sem=a2a_s.at[d], recv_sem=a2a_r.at[s],
            device_id=(d // gyn, d % gyn), device_id_type=MESH,
        )

    def send(rel, carry):
        exchange((me + rel) % count, me).start()
        return carry

    lax.fori_loop(1, count, send, 0)
    recv[me] = part[me]

    for copy in small:
        copy.wait()
    x_table.wait()
    row = lax.broadcasted_iota(jnp.int32, (levels, strip, band), 1) + gx * strip
    wind[pl.ds(0, levels)] = jnp.where(row == gxn * strip - 1, 0.0, east[...])
    col = lax.broadcasted_iota(jnp.int32, (levels, strip, band), 2) + gy * band
    wind[pl.ds(levels, levels)] = jnp.where(col == gyn * band - 1, 0.0, north[...])

    for side in range(2):
        for k in range(2):
            r = (strip - 2 if side == 0 else 0) + k
            edge[side, k, pl.ds(0, fields)] = field[:, r, :]
            edge[side, k, pl.ds(fields, 2 * levels)] = wind[:, r, :]

    def halo_copy(side, dy):
        peer = gx + 1 if side == 0 else gx - 1
        return pltpu.make_async_remote_copy(
            src_ref=edge.at[side], dst_ref=halo.at[side, dy],
            send_sem=halo_s.at[side, dy], recv_sem=halo_r.at[side, dy],
            device_id=(peer, (gy + dy) % gyn), device_id_type=MESH,
        )

    for dy in range(2):

        @pl.when(gx < gxn - 1)
        def _():
            halo_copy(0, dy).start()

        @pl.when(gx > 0)
        def _():
            halo_copy(1, dy).start()

        @pl.when(gx == 0)
        def _():
            halo[0, dy] = jnp.zeros(halo.shape[2:], jnp.float32)

        @pl.when(gx == gxn - 1)
        def _():
            halo[1, dy] = jnp.zeros(halo.shape[2:], jnp.float32)

    for b in range((fields + 2 * levels) // 8):
        if b * 8 < fields:
            block = field[pl.ds(b * 8, 8)]
        else:
            block = wind[pl.ds(b * 8 - fields, 8)]
        turned = block.reshape(8 * strip, band).T
        ysend[b] = jnp.where(gy == 0, turned[band - 8 :], turned[:8])
    ycopy = pltpu.make_async_remote_copy(
        src_ref=ysend, dst_ref=ytile, send_sem=y_s, recv_sem=y_r,
        device_id=(gx, 1 - gy), device_id_type=MESH,
    )
    ycopy.start()

    def receive(rel, carry):
        exchange((me + rel) % count, (me + rel) % count).wait_recv()
        return carry

    lax.fori_loop(1, count, receive, 0)
    rhs = jnp.concatenate(
        [recv[:, j].reshape(count * strip // 2, 2 * MY) for j in range(own)], axis=1
    )
    high, low = split(rhs)
    modes = dot(wx[0], high) + (dot(wx[0], low) + dot(wx[1], high))
    z, y, c, x = gx // 4, (gx // 2) % 2, gx % 2, gy
    hm = MX // 2
    lane = lax.broadcasted_iota(jnp.int32, (hm, 2 * MY), 1)
    for j in range(own):
        q = modes[:, j * 2 * MY : (j + 1) * 2 * MY]
        even = q[:hm] + pltpu.roll(q[2 * hm : 3 * hm], MY, 1)
        odd = pltpu.roll(q[hm : 2 * hm], MY, 1) + q[3 * hm :]
        coef[z, y, c, x, pl.ds(j * hm, hm)] = jnp.where(lane < MY, even, odd)

    part_rows = own * hm // 2
    first, second = pl.ds(0, part_rows), pl.ds(part_rows, part_rows)
    zs = [(z + k) % 4 for k in range(4)]

    def z_copy(k, slot):
        there = coef.at[slot, y, c, x]
        return pltpu.make_async_remote_copy(
            src_ref=there, dst_ref=there, send_sem=z_s.at[k], recv_sem=z_r.at[slot],
            device_id=(zs[k] * 4 + y * 2 + c, gy), device_id_type=MESH,
        )

    def to_x(ref, s, r):
        return pltpu.make_async_remote_copy(
            src_ref=ref, dst_ref=ref, send_sem=s, recv_sem=r,
            device_id=(gx, 1 - gy), device_id_type=MESH,
        )

    def to_y(ref, s, r):
        return pltpu.make_async_remote_copy(
            src_ref=ref, dst_ref=ref, send_sem=s, recv_sem=r,
            device_id=(z * 4 + (1 - y) * 2 + c, gy), device_id_type=MESH,
        )

    def to_core(ref, s, r):
        return pltpu.make_async_remote_copy(
            src_ref=ref, dst_ref=ref, send_sem=s, recv_sem=r,
            device_id=(z * 4 + y * 2 + 1 - c, gy), device_id_type=MESH,
        )

    def second_a(k, xx):
        return to_x(coef.at[zs[k], y, c, xx, first], p2_s.at[0, k], p2_r.at[0, zs[k]])

    def second_b(k, yy):
        return to_y(coef.at[zs[k], yy, c, x, second], p2_s.at[1, k], p2_r.at[1, zs[k]])

    def third_a(k, yy):
        return to_y(coef.at[zs[k], yy, c, :, first], p3_s.at[0, k], p3_r.at[0, zs[k]])

    def third_b(k, xx):
        return to_x(coef.at[zs[k], :, c, xx, second], p3_s.at[1, k], p3_r.at[1, zs[k]])

    def core_copy(k, cc):
        return to_core(coef.at[zs[k], :, cc], core_s.at[k], core_r.at[zs[k]])

    for k in range(1, 4):
        z_copy(k, z).start()
    second_a(0, x).start()
    second_b(0, y).start()

    for f in range(fields):
        full[0, pl.ds(f * ext, strip)] = field[f]
    for f in range(2 * levels):
        full[0, pl.ds((fields + f) * ext, strip)] = wind[f]
    blank = jnp.zeros((total, band), jnp.float32)
    ycopy.wait()
    for dy in range(2):

        @pl.when(gx < gxn - 1)
        def _():
            halo_copy(0, dy).wait_send()
            halo_copy(1, dy).wait_recv()

        @pl.when(gx > 0)
        def _():
            halo_copy(1, dy).wait_send()
            halo_copy(0, dy).wait_recv()

    for d in range(2):
        for k in range(2):
            full[d, pl.ds(strip + k, total, stride=ext), :] = halo[1, d, k]
            full[d, pl.ds(strip + 6 + k, total, stride=ext), :] = halo[0, d, k]
        for k in range(2, 6):
            full[d, pl.ds(strip + k, total, stride=ext), :] = blank

    for k in range(1, 4):
        z_copy(k, zs[k]).wait_recv()
        second_a(k, x).start()
        second_b(k, y).start()

    gap = jnp.zeros((band - 16, 8 * strip), jnp.float32)
    for b in range(total // 8):
        tile = ytile[b]
        spread = jnp.concatenate(
            [jnp.where(gy == 0, tile, 0.0), gap, jnp.where(gy == 1, tile, 0.0)], axis=0
        )
        turned = spread.T
        for i in range(8):
            full[1, pl.ds((b * 8 + i) * ext, strip)] = turned[i * strip : (i + 1) * strip]

    for k in range(4):
        second_a(k, 1 - x).wait_recv()
        second_b(k, 1 - y).wait_recv()
        third_a(k, y).start()
        third_b(k, x).start()

    def extended(f):
        rows = pl.ds(pl.multiple_of(f * ext, 8), ext)
        return jnp.concatenate([full[0, rows], full[1, rows]], axis=1)

    for lev in range(levels):
        u, v = extended(fields + lev), extended(fields + levels + lev)
        winds[lev, 0] = jnp.maximum(u, 0.0)
        winds[lev, 1] = jnp.minimum(u, 0.0)
        winds[lev, 2] = jnp.maximum(v, 0.0)
        winds[lev, 3] = jnp.minimum(v, 0.0)

    lane = lax.broadcasted_iota(jnp.int32, (ext, 2 * MY), 1)

    def store(src, dst, slot, index):
        rows = pl.ds(pl.multiple_of(slot * (fields // 4), 8), fields // 4)
        return pltpu.make_async_copy(src.at[rows], dst.at[rows], stores.at[index, slot])

    def compute(slot):
        base = slot * (fields // 4)

        def inverse(i, carry):
            rows = coef.at[slot, i // 4, (i // 2) % 2, i % 2]
            blocks = [rows[pl.ds(j * hm, hm)] for j in range(own)]
            for j in range(own):
                flat[pl.ds(pl.multiple_of((i * own + j) * hm, hm), hm)] = blocks[j]
            joined = jnp.concatenate(blocks, axis=1)
            high, low = split(joined)
            mixed = dot(xb[...], jnp.concatenate([high, low, high], axis=0))
            stack = []
            for j in range(own):
                one = mixed[:, j * 2 * MY : (j + 1) * 2 * MY]
                stack.append(jnp.where(lane < MY, one[:ext], one[ext:]))
            high, low = split(jnp.concatenate(stack, axis=0))
            got = dot(high, wi[0]) + (dot(low, wi[0]) + dot(high, wi[1]))
            large[pl.ds(i * own, own)] = got.reshape(own, ext, gyn * band)
            return carry

        lax.fori_loop(0, fields // own // 4, inverse, 0, unroll=4)
        held = pl.ds(pl.multiple_of(base, 8), fields // 4)
        for j in range(hm):
            packed[held, pl.ds(j * 2 * MY, 2 * MY)] = flat[pl.ds(j, fields // 4, stride=hm), :]
        store(packed, coef_out, slot, 1).start()

        def tracer(i, carry):
            f = base + i
            lev = f % levels
            up, un, vp, vn = winds[lev, 0], winds[lev, 1], winds[lev, 2], winds[lev, 3]
            q = extended(f) + large[i]
            for _ in range(2):
                flux = up * q + un * pltpu.roll(q, ext - 1, 0)
                cross = vp * q + vn * pltpu.roll(q, gyn * band - 1, 1)
                q = q - (flux - pltpu.roll(flux, 1, 0))
                q = q - (cross - pltpu.roll(cross, 1, 1))
            out[f] = q[:strip, :band]
            return carry

        lax.fori_loop(0, fields // 4, tracer, 0, unroll=6)
        store(out, advected, slot, 0).start()

    for k in range(4):
        third_a(k, 1 - y).wait_recv()
        third_b(k, 1 - x).wait_recv()
        core_copy(k, c).start()
        if k:
            core_copy(k - 1, 1 - c).wait_recv()
            compute(zs[k - 1])
    core_copy(3, 1 - c).wait_recv()
    compute(zs[3])

    for k in range(1, 4):
        z_copy(k, z).wait_send()
    for k in range(4):
        second_a(k, x).wait_send()
        second_b(k, y).wait_send()
        third_a(k, y).wait_send()
        third_b(k, x).wait_send()
        core_copy(k, c).wait_send()

    def drain(rel, carry):
        exchange((me + rel) % count, me).wait_send()
        return carry

    lax.fori_loop(1, count, drain, 0)
    for k in range(4):
        store(out, advected, zs[k], 0).wait()
        store(packed, coef_out, zs[k], 1).wait()


def fused(field, driver, east, north):
    tracers, levels, strip, band = field.shape
    gxn, gyn = lax.axis_size("gx"), lax.axis_size("gy")
    count = gxn * gyn
    fields = tracers * levels
    own = fields // count
    total = fields + 2 * levels
    wy, wx, xb, wi = tables(gxn, gyn, strip, band)
    flat = field.reshape(fields, strip, band)
    dma = pltpu.SemaphoreType.DMA
    f32 = jnp.float32
    bf16 = jnp.bfloat16
    hbm = pl.BlockSpec(memory_space=pltpu.HBM)
    coeffs, advected = pl.pallas_call(
        spectral_kernel,
        out_shape=(
            jax.ShapeDtypeStruct((fields, MX * MY), f32),
            jax.ShapeDtypeStruct((fields, strip, band), f32),
        ),
        in_specs=[hbm] * 8,
        out_specs=(hbm, hbm),
        scratch_shapes=[
            pltpu.VMEM((4, 2, 2, 2, own * MX // 2, 2 * MY), f32),
            pltpu.VMEM((fields, strip, band), f32),
            pltpu.VMEM((fields, MX * MY), f32),
            pltpu.VMEM((fields // 4 * MX // 2, 2 * MY), f32),
            dma((2, 4)),
            pltpu.VMEM((fields, strip, band), f32),
            pltpu.VMEM((fields, strip, band), f32),
            pltpu.VMEM((levels, strip, band), f32),
            pltpu.VMEM((levels, strip, band), f32),
            pltpu.VMEM(wy.shape[1:], bf16),
            pltpu.VMEM(wx.shape, bf16),
            pltpu.VMEM(xb.shape[1:], bf16),
            pltpu.VMEM(wi.shape[1:], bf16),
            pltpu.VMEM((count, own, strip // 2, 2 * MY), f32),
            pltpu.VMEM((count, own, strip // 2, 2 * MY), f32),
            pltpu.VMEM((2, 2, total, band), f32),
            pltpu.VMEM((total // 8, 8, 8 * strip), f32),
            pltpu.VMEM((2 * levels, strip, band), f32),
            pltpu.VMEM((2, 2, 2, total, band), f32),
            pltpu.VMEM((total // 8, 8, 8 * strip), f32),
            pltpu.VMEM((gyn, total * (strip + 8), band), f32),
            pltpu.VMEM((levels, 4, strip + 8, gyn * band), f32),
            pltpu.VMEM((fields // 4, strip + 8, gyn * band), f32),
            dma((6 + 2 * (fields // (4 * own)),)),
            dma((count,)), dma((count,)), dma((2, 2)), dma((2, 2)), dma, dma,
            dma((4,)), dma((4,)), dma((2, 4)), dma((2, 4)), dma((2, 4)), dma((2, 4)),
            dma((4,)), dma((4,)),
        ],
        compiler_params=pltpu.CompilerParams(
            collective_id=0, has_side_effects=True, vmem_limit_bytes=62 << 20
        ),
        name="spectral",
    )(
        flat, driver.reshape(fields, strip, band), east, north,
        jnp.asarray(wy), jnp.asarray(wx), jnp.asarray(xb), jnp.asarray(wi),
    )
    return (
        advected.reshape(tracers, levels, strip, band),
        coeffs.reshape(tracers, levels, MX * MY),
    )


def body(field, driver, east, north):
    tracers, levels, strip, band = field.shape
    sizes = (lax.axis_size("gx"), lax.axis_size("gy"))
    if sizes == (16, 2) and (tracers * levels, levels, strip, band) == (96, 16, 16, 128):
        return fused(field, driver, east, north)
    return shards(field, driver, east, north)


def solution(mesh):
    placed = (
        P(None, None, "gx", "gy"),
        P(None, None, "gx", "gy"),
        P(None, "gx", "gy"),
        P(None, "gx", "gy"),
    )
    return jax.shard_map(
        body,
        mesh=mesh,
        in_specs=placed,
        out_specs=(P(None, None, "gx", "gy"), P()),
        check_vma=False,
    )
```

```python
import math

import jax
import jax.numpy as jnp
import ml_dtypes
import numpy as np
from jax import lax
from jax.experimental import pallas as pl
from jax.experimental.pallas import tpu as pltpu
from jax.sharding import PartitionSpec as P

MX = 64
MY = 64
MESH = pl.DeviceIdType.MESH


def shifted(value, axis, steps):
    count = lax.axis_size(axis)
    first, last = (max(0, -steps), min(count, count - steps))
    return lax.ppermute(value, axis, [(source, source + steps) for source in range(first, last)])


def padded(x, sides, width):
    for axis, dim in sides:
        peers, length = (lax.axis_size(axis), x.shape[dim])
        up = [(i, (i + 1) % peers) for i in range(peers - 1)]
        down = [(j, i) for i, j in up]
        last = lax.slice_in_dim(x, length - width, length, axis=dim)
        first = lax.slice_in_dim(x, 0, width, axis=dim)
        before = lax.ppermute(last, axis, up)
        after = lax.ppermute(first, axis, down)
        x = jnp.concatenate([before, x, after], axis=dim)
    return x


def cosine_table(first, count, total, modes):
    indices = first + jnp.arange(count, dtype=jnp.int32)
    wavenum = jnp.arange(modes, dtype=jnp.int32)
    phases = (wavenum[None, :] * (2 * indices[:, None] + 1)).astype(jnp.float32)
    cosines = jnp.cos(phases * (math.pi / (2.0 * total)))
    weight = jnp.where(wavenum == 0, math.sqrt(1.0 / total), math.sqrt(2.0 / total)).astype(
        jnp.float32
    )
    return cosines * weight[None, :]


def upwind(tracer, winds):
    east = winds[0]
    north = winds[1]
    east_flux = (
        jnp.maximum(east[:, :-1, :], 0.0) * tracer[..., :-1, :]
        + jnp.minimum(east[:, :-1, :], 0.0) * tracer[..., 1:, :]
    )
    north_flux = (
        jnp.maximum(north[:, :, :-1], 0.0) * tracer[..., :, :-1]
        + jnp.minimum(north[:, :, :-1], 0.0) * tracer[..., :, 1:]
    )
    inner = tracer[..., 1:-1, 1:-1]
    inner = inner - (east_flux[..., 1:, 1:-1] - east_flux[..., :-1, 1:-1])
    return inner - (north_flux[..., 1:-1, 1:] - north_flux[..., 1:-1, :-1])


def shards(field, driver, east_wind, north_wind):
    high = lax.Precision.HIGHEST
    tracers, levels, strip_cols, band_rows = field.shape
    nx_total = strip_cols * lax.axis_size("gx")
    ny_total = band_rows * lax.axis_size("gy")
    x_first = lax.axis_index("gx") * strip_cols
    y_first = lax.axis_index("gy") * band_rows
    x_table = cosine_table(x_first, strip_cols, nx_total, MX)
    y_table = cosine_table(y_first, band_rows, ny_total, MY)
    departure = driver - field
    half_proj = jnp.einsum("tlxy,xm->tlmy", departure, x_table, precision=high)
    partial_modes = jnp.einsum("tlmy,yn->tlmn", half_proj, y_table, precision=high)
    partial_modes = partial_modes.reshape(tracers, levels, MX * MY)
    coeffs = lax.psum(partial_modes, ("gx", "gy"))
    modal = coeffs.reshape(tracers, levels, MX, MY)
    large_scale = jnp.einsum("tlmn,yn->tlmy", modal, y_table, precision=high)
    large_scale = jnp.einsum("tlmy,xm->tlxy", large_scale, x_table, precision=high)
    nudged = field + 0.5 * large_scale
    xpos = x_first + jnp.arange(strip_cols, dtype=jnp.int32)
    ypos = y_first + jnp.arange(band_rows, dtype=jnp.int32)
    east_face = jnp.where(xpos[None, :, None] == nx_total - 1, jnp.float32(0.0), east_wind)
    north_face = jnp.where(ypos[None, None, :] == ny_total - 1, jnp.float32(0.0), north_wind)
    east_below = shifted(east_face[:, -1:, :], "gx", 1)
    north_below = shifted(north_face[:, :, -1:], "gy", 1)
    east_ext = jnp.concatenate([east_below, east_face, jnp.zeros_like(east_below)], axis=1)
    east_ext = jnp.pad(east_ext, ((0, 0), (0, 0), (1, 1)))
    north_ext = jnp.concatenate([north_below, north_face, jnp.zeros_like(north_below)], axis=2)
    north_ext = jnp.pad(north_ext, ((0, 0), (1, 1), (0, 0)))
    wind_ext = jnp.stack([east_ext, north_ext])
    advected = nudged
    for sweep in range(2):
        field_ext = padded(advected, (("gx", 2), ("gy", 3)), 1)
        advected = upwind(field_ext, wind_ext)
    return (advected, coeffs)


def split(value):
    high = value.astype(jnp.bfloat16)
    return high, (value - high.astype(jnp.float32)).astype(jnp.bfloat16)


def split_table(table):
    table = np.asarray(table, np.float32)
    high = table.astype(ml_dtypes.bfloat16)
    low = (table - high.astype(np.float32)).astype(ml_dtypes.bfloat16)
    return high, low


def table64(total, modes):
    index = np.arange(total)[:, None]
    wave = np.arange(modes)[None, :]
    weight = np.where(wave == 0, math.sqrt(1.0 / total), math.sqrt(2.0 / total))
    turns = (wave * (2 * index + 1)) % (4 * total)
    return np.cos(turns * (math.pi / (2.0 * total))) * weight


def dot(a, b):
    return jnp.dot(a, b, preferred_element_type=jnp.float32)


def tables(gxn, gyn, strip, band):
    bx = table64(gxn * strip, MX)
    by = table64(gyn * band, MY)
    half = strip // 2
    forward_y = np.zeros((gyn, 2 * band, 2 * MY))
    for g in range(gyn):
        own = by[g * band : (g + 1) * band]
        forward_y[g, :band, :MY] = own
        forward_y[g, band:, MY:] = own
    wy = np.stack(split_table(forward_y), axis=1)
    bx4 = bx.reshape(gxn, 2, half, MX // 2, 2)
    forward_x = np.broadcast_to(
        bx4.transpose(1, 4, 3, 0, 2)[:, :, :, :, None, :], (2, 2, MX // 2, gxn, gyn, half)
    )
    wx = np.stack(split_table(forward_x.reshape(2 * MX, gxn * gyn * half)))
    inverse_x = np.zeros((gxn, 2, strip + 8, MX // 2))
    for g in range(gxn):
        for row in range(strip + 8):
            if row < strip + 2:
                x = g * strip + row
            elif row >= strip + 6:
                x = g * strip + row - strip - 8
            else:
                continue
            if 0 <= x < gxn * strip:
                inverse_x[g, :, row] = bx[x].reshape(MX // 2, 2).T
    high, low = split_table(inverse_x.reshape(gxn, 2 * (strip + 8), MX // 2))
    xb = np.concatenate([high, high, low], axis=2)
    inverse_y = np.zeros((gyn, 2 * MY, gyn * band))
    for g in range(gyn):
        rolled = 0.5 * np.roll(by, -g * band, axis=0).T
        inverse_y[g, :MY] = rolled
        inverse_y[g, MY:] = rolled
    wi = np.stack(split_table(inverse_y), axis=1)
    return wy, wx, xb, wi


def spectral_kernel(
    field_in, driver_in, east_in, north_in, wy_in, wx_in, xb_in, wi_in, coef_out, advected,
    coef, out, packed, flat, stores, field, driver, east, north, wy, wx, xb, wi,
    part, recv, edge, ysend, wind, halo, ytile, full, winds, large, loads,
    a2a_s, a2a_r, halo_s, halo_r, y_s, y_r, z_s, z_r, p2_s, p2_r, p3_s, p3_r, core_s, core_r,
):
    gx = lax.axis_index("gx")
    gy = lax.axis_index("gy")
    gxn, gyn = lax.axis_size("gx"), lax.axis_size("gy")
    count = gxn * gyn
    me = gx * gyn + gy
    fields, strip, band = field.shape
    levels = east.shape[0]
    own = fields // count
    ext = strip + 8
    total = fields + 2 * levels
    chunk = 4 * own
    chunks = fields // chunk

    def load(src, dst, index):
        return pltpu.make_async_copy(src, dst, loads.at[index])

    def piece(src, dst, c, index):
        rows = pl.ds(c * chunk, chunk)
        return load(src.at[rows], dst.at[rows], index)

    y_table = load(wy_in.at[gy], wy, 0)
    x_table = load(wx_in, wx, 1)
    small = [
        load(east_in, east, 2),
        load(north_in, north, 3),
        load(xb_in.at[gx], xb, 4),
        load(wi_in.at[gy], wi, 5),
    ]
    pieces = [
        (piece(field_in, field, c, 6 + c), piece(driver_in, driver, c, 6 + chunks + c))
        for c in range(chunks)
    ]
    y_table.start()
    for a, b in pieces:
        a.start()
        b.start()
    x_table.start()
    for copy in small:
        copy.start()

    barrier = pltpu.get_barrier_semaphore()

    def greet(rel, carry):
        d = (me + rel) % count
        pl.semaphore_signal(
            barrier, inc=1, device_id=(d // gyn, d % gyn), device_id_type=MESH
        )
        return carry

    lax.fori_loop(1, count, greet, 0)

    y_table.wait()
    wh, wl = wy[0], wy[1]
    for c in range(chunks):
        pieces[c][0].wait()
        pieces[c][1].wait()
        rows = pl.ds(c * chunk, chunk)
        departure = driver[rows] - field[rows]
        lhs = jnp.concatenate([departure[:, : strip // 2], departure[:, strip // 2 :]], axis=2)
        high, low = split(lhs.reshape(chunk * strip // 2, 2 * band))
        got = dot(high, wh) + (dot(low, wh) + dot(high, wl))
        part[pl.ds(c * 4, 4)] = got.reshape(4, own, strip // 2, 2 * MY)
    pl.semaphore_wait(barrier, count - 1)

    def exchange(d, s):
        return pltpu.make_async_remote_copy(
            src_ref=part.at[d], dst_ref=recv.at[s], send_sem=a2a_s.at[d], recv_sem=a2a_r.at[s],
            device_id=(d // gyn, d % gyn), device_id_type=MESH,
        )

    def send(rel, carry):
        exchange((me + rel) % count, me).start()
        return carry

    lax.fori_loop(1, count, send, 0)
    recv[me] = part[me]

    for copy in small:
        copy.wait()
    x_table.wait()
    row = lax.broadcasted_iota(jnp.int32, (levels, strip, band), 1) + gx * strip
    wind[pl.ds(0, levels)] = jnp.where(row == gxn * strip - 1, 0.0, east[...])
    col = lax.broadcasted_iota(jnp.int32, (levels, strip, band), 2) + gy * band
    wind[pl.ds(levels, levels)] = jnp.where(col == gyn * band - 1, 0.0, north[...])

    for side in range(2):
        for k in range(2):
            r = (strip - 2 if side == 0 else 0) + k
            edge[side, k, pl.ds(0, fields)] = field[:, r, :]
            edge[side, k, pl.ds(fields, 2 * levels)] = wind[:, r, :]

    def halo_copy(side, dy):
        peer = gx + 1 if side == 0 else gx - 1
        return pltpu.make_async_remote_copy(
            src_ref=edge.at[side], dst_ref=halo.at[side, dy],
            send_sem=halo_s.at[side, dy], recv_sem=halo_r.at[side, dy],
            device_id=(peer, gy), device_id_type=MESH,
        )

    @pl.when(gx < gxn - 1)
    def _():
        halo_copy(0, 0).start()

    @pl.when(gx > 0)
    def _():
        halo_copy(1, 0).start()

    @pl.when(gx == 0)
    def _():
        halo[0, 0] = jnp.zeros(halo.shape[2:], jnp.float32)

    @pl.when(gx == gxn - 1)
    def _():
        halo[1, 0] = jnp.zeros(halo.shape[2:], jnp.float32)

    for b in range((fields + 2 * levels) // 8):
        if b * 8 < fields:
            block = field[pl.ds(b * 8, 8)]
        else:
            block = wind[pl.ds(b * 8 - fields, 8)]
        turned = block.reshape(8 * strip, band).T
        ysend[b] = jnp.where(gy == 0, turned[band - 8 :], turned[:8])
    ycopy = pltpu.make_async_remote_copy(
        src_ref=ysend, dst_ref=ytile, send_sem=y_s, recv_sem=y_r,
        device_id=(gx, 1 - gy), device_id_type=MESH,
    )

    def receive(rel, carry):
        exchange((me + rel) % count, (me + rel) % count).wait_recv()
        return carry

    lax.fori_loop(1, count, receive, 0)
    rhs = jnp.concatenate(
        [recv[:, j].reshape(count * strip // 2, 2 * MY) for j in range(own)], axis=1
    )
    high, low = split(rhs)
    modes = dot(wx[0], high) + (dot(wx[0], low) + dot(wx[1], high))
    z, y, c, x = gx // 4, (gx // 2) % 2, gx % 2, gy
    hm = MX // 2
    lane = lax.broadcasted_iota(jnp.int32, (hm, 2 * MY), 1)
    for j in range(own):
        q = modes[:, j * 2 * MY : (j + 1) * 2 * MY]
        even = q[:hm] + pltpu.roll(q[2 * hm : 3 * hm], MY, 1)
        odd = pltpu.roll(q[hm : 2 * hm], MY, 1) + q[3 * hm :]
        coef[z, y, c, x, pl.ds(j * hm, hm)] = jnp.where(lane < MY, even, odd)

    part_rows = own * hm // 2
    first, second = pl.ds(0, part_rows), pl.ds(part_rows, part_rows)
    zs = [(z + k) % 4 for k in range(4)]

    def z_copy(k, slot):
        there = coef.at[slot, y, c, x]
        return pltpu.make_async_remote_copy(
            src_ref=there, dst_ref=there, send_sem=z_s.at[k], recv_sem=z_r.at[slot],
            device_id=(zs[k] * 4 + y * 2 + c, gy), device_id_type=MESH,
        )

    def to_x(ref, s, r):
        return pltpu.make_async_remote_copy(
            src_ref=ref, dst_ref=ref, send_sem=s, recv_sem=r,
            device_id=(gx, 1 - gy), device_id_type=MESH,
        )

    def to_y(ref, s, r):
        return pltpu.make_async_remote_copy(
            src_ref=ref, dst_ref=ref, send_sem=s, recv_sem=r,
            device_id=(z * 4 + (1 - y) * 2 + c, gy), device_id_type=MESH,
        )

    def to_core(ref, s, r):
        return pltpu.make_async_remote_copy(
            src_ref=ref, dst_ref=ref, send_sem=s, recv_sem=r,
            device_id=(z * 4 + y * 2 + 1 - c, gy), device_id_type=MESH,
        )

    def second_a(k, xx):
        return to_x(coef.at[zs[k], y, c, xx, first], p2_s.at[0, k], p2_r.at[0, zs[k]])

    def second_b(k, yy):
        return to_y(coef.at[zs[k], yy, c, x, second], p2_s.at[1, k], p2_r.at[1, zs[k]])

    def third_a(k, yy):
        return to_y(coef.at[zs[k], yy, c, :, first], p3_s.at[0, k], p3_r.at[0, zs[k]])

    def third_b(k, xx):
        return to_x(coef.at[zs[k], :, c, xx, second], p3_s.at[1, k], p3_r.at[1, zs[k]])

    def core_copy(k, cc):
        return to_core(coef.at[zs[k], :, cc], core_s.at[k], core_r.at[zs[k]])

    for k in range(1, 4):
        z_copy(k, z).start()
    second_a(0, x).start()
    second_b(0, y).start()

    @pl.when(gx < gxn - 1)
    def _():
        halo_copy(0, 0).wait_send()
        halo_copy(1, 0).wait_recv()

    @pl.when(gx > 0)
    def _():
        halo_copy(1, 0).wait_send()
        halo_copy(0, 0).wait_recv()

    blocks_y = total // 8
    for h in range(2):
        for k in range(2):
            turned = halo[h, 0, k].T
            ysend[blocks_y + 2 * h + k] = jnp.where(gy == 0, turned[band - 8 :], turned[:8])
    ycopy.start()

    for f in range(fields):
        full[0, pl.ds(f * ext, strip)] = field[f]
    for f in range(2 * levels):
        full[0, pl.ds((fields + f) * ext, strip)] = wind[f]
    blank = jnp.zeros((total, band), jnp.float32)
    for k in range(2):
        full[0, pl.ds(strip + k, total, stride=ext), :] = halo[1, 0, k]
        full[0, pl.ds(strip + 6 + k, total, stride=ext), :] = halo[0, 0, k]
    for d in range(2):
        for k in range(2, 6):
            full[d, pl.ds(strip + k, total, stride=ext), :] = blank
    gap = jnp.zeros((band - 16, 8 * strip), jnp.float32)

    def turn(b):
        tile = ytile[b]
        return jnp.concatenate(
            [jnp.where(gy == 0, tile, 0.0), gap, jnp.where(gy == 1, tile, 0.0)], axis=0
        ).T

    def assemble():
        ycopy.wait()
        for b in range(blocks_y):
            turned = turn(b)
            for i in range(8):
                full[1, pl.ds((b * 8 + i) * ext, strip)] = turned[i * strip : (i + 1) * strip]
        for k in range(2):
            full[1, pl.ds(strip + k, total, stride=ext), :] = turn(blocks_y + 2 + k)
            full[1, pl.ds(strip + 6 + k, total, stride=ext), :] = turn(blocks_y + k)
        for lev in range(levels):
            u, v = extended(fields + lev), extended(fields + levels + lev)
            winds[lev, 0] = jnp.maximum(u, 0.0)
            winds[lev, 1] = jnp.minimum(u, 0.0)
            winds[lev, 2] = jnp.maximum(v, 0.0)
            winds[lev, 3] = jnp.minimum(v, 0.0)

    def extended(f):
        rows = pl.ds(pl.multiple_of(f * ext, 8), ext)
        return jnp.concatenate([full[0, rows], full[1, rows]], axis=1)

    lane = lax.broadcasted_iota(jnp.int32, (ext, 2 * MY), 1)

    def store(src, dst, slot, index):
        rows = pl.ds(pl.multiple_of(slot * (fields // 4), 8), fields // 4)
        return pltpu.make_async_copy(src.at[rows], dst.at[rows], stores.at[index, slot])

    def compute(slot):
        base = slot * (fields // 4)

        def inverse(i, carry):
            rows = coef.at[slot, i // 4, (i // 2) % 2, i % 2]
            blocks = [rows[pl.ds(j * hm, hm)] for j in range(own)]
            for j in range(own):
                flat[pl.ds(pl.multiple_of((i * own + j) * hm, hm), hm)] = blocks[j]
            joined = jnp.concatenate(blocks, axis=1)
            high, low = split(joined)
            mixed = dot(xb[...], jnp.concatenate([high, low, high], axis=0))
            stack = []
            for j in range(own):
                one = mixed[:, j * 2 * MY : (j + 1) * 2 * MY]
                stack.append(jnp.where(lane < MY, one[:ext], one[ext:]))
            high, low = split(jnp.concatenate(stack, axis=0))
            got = dot(high, wi[0]) + (dot(low, wi[0]) + dot(high, wi[1]))
            large[pl.ds(i * own, own)] = got.reshape(own, ext, gyn * band)
            return carry

        lax.fori_loop(0, fields // own // 4, inverse, 0, unroll=4)
        held = pl.ds(pl.multiple_of(base, 8), fields // 4)
        for j in range(hm):
            packed[held, pl.ds(j * 2 * MY, 2 * MY)] = flat[pl.ds(j, fields // 4, stride=hm), :]
        store(packed, coef_out, slot, 1).start()

        def tracer(i, carry):
            f = base + i
            lev = f % levels
            up, un, vp, vn = winds[lev, 0], winds[lev, 1], winds[lev, 2], winds[lev, 3]
            q = extended(f) + large[i]
            for _ in range(2):
                flux = up * q + un * pltpu.roll(q, ext - 1, 0)
                cross = vp * q + vn * pltpu.roll(q, gyn * band - 1, 1)
                q = q - (flux - pltpu.roll(flux, 1, 0))
                q = q - (cross - pltpu.roll(cross, 1, 1))
            out[f] = q[:strip, :band]
            return carry

        lax.fori_loop(0, fields // 4, tracer, 0, unroll=6)
        store(out, advected, slot, 0).start()

    for step in range(1, 7):
        if step < 4:
            z_copy(step, zs[step]).wait_recv()
            second_a(step, x).start()
            second_b(step, y).start()
        k = step - 1
        if k < 4:
            second_a(k, 1 - x).wait_recv()
            second_b(k, 1 - y).wait_recv()
            third_a(k, y).start()
            third_b(k, x).start()
        k = step - 2
        if 0 <= k < 4:
            third_a(k, 1 - y).wait_recv()
            third_b(k, 1 - x).wait_recv()
            core_copy(k, c).start()
        if step == 2:
            assemble()
        k = step - 3
        if k >= 0:
            core_copy(k, 1 - c).wait_recv()
            compute(zs[k])

    for k in range(1, 4):
        z_copy(k, z).wait_send()
    for k in range(4):
        second_a(k, x).wait_send()
        second_b(k, y).wait_send()
        third_a(k, y).wait_send()
        third_b(k, x).wait_send()
        core_copy(k, c).wait_send()

    def drain(rel, carry):
        exchange((me + rel) % count, me).wait_send()
        return carry

    lax.fori_loop(1, count, drain, 0)
    for k in range(4):
        store(out, advected, zs[k], 0).wait()
        store(packed, coef_out, zs[k], 1).wait()


def fused(field, driver, east, north):
    tracers, levels, strip, band = field.shape
    gxn, gyn = lax.axis_size("gx"), lax.axis_size("gy")
    count = gxn * gyn
    fields = tracers * levels
    own = fields // count
    total = fields + 2 * levels
    wy, wx, xb, wi = tables(gxn, gyn, strip, band)
    flat = field.reshape(fields, strip, band)
    dma = pltpu.SemaphoreType.DMA
    f32 = jnp.float32
    bf16 = jnp.bfloat16
    hbm = pl.BlockSpec(memory_space=pltpu.HBM)
    coeffs, advected = pl.pallas_call(
        spectral_kernel,
        out_shape=(
            jax.ShapeDtypeStruct((fields, MX * MY), f32),
            jax.ShapeDtypeStruct((fields, strip, band), f32),
        ),
        in_specs=[hbm] * 8,
        out_specs=(hbm, hbm),
        scratch_shapes=[
            pltpu.VMEM((4, 2, 2, 2, own * MX // 2, 2 * MY), f32),
            pltpu.VMEM((fields, strip, band), f32),
            pltpu.VMEM((fields, MX * MY), f32),
            pltpu.VMEM((fields // 4 * MX // 2, 2 * MY), f32),
            dma((2, 4)),
            pltpu.VMEM((fields, strip, band), f32),
            pltpu.VMEM((fields, strip, band), f32),
            pltpu.VMEM((levels, strip, band), f32),
            pltpu.VMEM((levels, strip, band), f32),
            pltpu.VMEM(wy.shape[1:], bf16),
            pltpu.VMEM(wx.shape, bf16),
            pltpu.VMEM(xb.shape[1:], bf16),
            pltpu.VMEM(wi.shape[1:], bf16),
            pltpu.VMEM((count, own, strip // 2, 2 * MY), f32),
            pltpu.VMEM((count, own, strip // 2, 2 * MY), f32),
            pltpu.VMEM((2, 2, total, band), f32),
            pltpu.VMEM((total // 8 + 4, 8, 8 * strip), f32),
            pltpu.VMEM((2 * levels, strip, band), f32),
            pltpu.VMEM((2, 1, 2, total, band), f32),
            pltpu.VMEM((total // 8 + 4, 8, 8 * strip), f32),
            pltpu.VMEM((gyn, total * (strip + 8), band), f32),
            pltpu.VMEM((levels, 4, strip + 8, gyn * band), f32),
            pltpu.VMEM((fields // 4, strip + 8, gyn * band), f32),
            dma((6 + 2 * (fields // (4 * own)),)),
            dma((count,)), dma((count,)), dma((2, 1)), dma((2, 1)), dma, dma,
            dma((4,)), dma((4,)), dma((2, 4)), dma((2, 4)), dma((2, 4)), dma((2, 4)),
            dma((4,)), dma((4,)),
        ],
        compiler_params=pltpu.CompilerParams(
            collective_id=0, has_side_effects=True, vmem_limit_bytes=62 << 20
        ),
        name="spectral",
    )(
        flat, driver.reshape(fields, strip, band), east, north,
        jnp.asarray(wy), jnp.asarray(wx), jnp.asarray(xb), jnp.asarray(wi),
    )
    return (
        advected.reshape(tracers, levels, strip, band),
        coeffs.reshape(tracers, levels, MX * MY),
    )


def body(field, driver, east, north):
    tracers, levels, strip, band = field.shape
    sizes = (lax.axis_size("gx"), lax.axis_size("gy"))
    if sizes == (16, 2) and (tracers * levels, levels, strip, band) == (96, 16, 16, 128):
        return fused(field, driver, east, north)
    return shards(field, driver, east, north)


def solution(mesh):
    placed = (
        P(None, None, "gx", "gy"),
        P(None, None, "gx", "gy"),
        P(None, "gx", "gy"),
        P(None, "gx", "gy"),
    )
    return jax.shard_map(
        body,
        mesh=mesh,
        in_specs=placed,
        out_specs=(P(None, None, "gx", "gy"), P()),
        check_vma=False,
    )
```

```python
import math

import jax
import jax.numpy as jnp
import ml_dtypes
import numpy as np
from jax import lax
from jax.experimental import pallas as pl
from jax.experimental.pallas import tpu as pltpu
from jax.sharding import PartitionSpec as P

MX = 64
MY = 64
MESH = pl.DeviceIdType.MESH


def shifted(value, axis, steps):
    count = lax.axis_size(axis)
    first, last = (max(0, -steps), min(count, count - steps))
    return lax.ppermute(value, axis, [(source, source + steps) for source in range(first, last)])


def padded(x, sides, width):
    for axis, dim in sides:
        peers, length = (lax.axis_size(axis), x.shape[dim])
        up = [(i, (i + 1) % peers) for i in range(peers - 1)]
        down = [(j, i) for i, j in up]
        last = lax.slice_in_dim(x, length - width, length, axis=dim)
        first = lax.slice_in_dim(x, 0, width, axis=dim)
        before = lax.ppermute(last, axis, up)
        after = lax.ppermute(first, axis, down)
        x = jnp.concatenate([before, x, after], axis=dim)
    return x


def cosine_table(first, count, total, modes):
    indices = first + jnp.arange(count, dtype=jnp.int32)
    wavenum = jnp.arange(modes, dtype=jnp.int32)
    phases = (wavenum[None, :] * (2 * indices[:, None] + 1)).astype(jnp.float32)
    cosines = jnp.cos(phases * (math.pi / (2.0 * total)))
    weight = jnp.where(wavenum == 0, math.sqrt(1.0 / total), math.sqrt(2.0 / total)).astype(
        jnp.float32
    )
    return cosines * weight[None, :]


def upwind(tracer, winds):
    east = winds[0]
    north = winds[1]
    east_flux = (
        jnp.maximum(east[:, :-1, :], 0.0) * tracer[..., :-1, :]
        + jnp.minimum(east[:, :-1, :], 0.0) * tracer[..., 1:, :]
    )
    north_flux = (
        jnp.maximum(north[:, :, :-1], 0.0) * tracer[..., :, :-1]
        + jnp.minimum(north[:, :, :-1], 0.0) * tracer[..., :, 1:]
    )
    inner = tracer[..., 1:-1, 1:-1]
    inner = inner - (east_flux[..., 1:, 1:-1] - east_flux[..., :-1, 1:-1])
    return inner - (north_flux[..., 1:-1, 1:] - north_flux[..., 1:-1, :-1])


def shards(field, driver, east_wind, north_wind):
    high = lax.Precision.HIGHEST
    tracers, levels, strip_cols, band_rows = field.shape
    nx_total = strip_cols * lax.axis_size("gx")
    ny_total = band_rows * lax.axis_size("gy")
    x_first = lax.axis_index("gx") * strip_cols
    y_first = lax.axis_index("gy") * band_rows
    x_table = cosine_table(x_first, strip_cols, nx_total, MX)
    y_table = cosine_table(y_first, band_rows, ny_total, MY)
    departure = driver - field
    half_proj = jnp.einsum("tlxy,xm->tlmy", departure, x_table, precision=high)
    partial_modes = jnp.einsum("tlmy,yn->tlmn", half_proj, y_table, precision=high)
    partial_modes = partial_modes.reshape(tracers, levels, MX * MY)
    coeffs = lax.psum(partial_modes, ("gx", "gy"))
    modal = coeffs.reshape(tracers, levels, MX, MY)
    large_scale = jnp.einsum("tlmn,yn->tlmy", modal, y_table, precision=high)
    large_scale = jnp.einsum("tlmy,xm->tlxy", large_scale, x_table, precision=high)
    nudged = field + 0.5 * large_scale
    xpos = x_first + jnp.arange(strip_cols, dtype=jnp.int32)
    ypos = y_first + jnp.arange(band_rows, dtype=jnp.int32)
    east_face = jnp.where(xpos[None, :, None] == nx_total - 1, jnp.float32(0.0), east_wind)
    north_face = jnp.where(ypos[None, None, :] == ny_total - 1, jnp.float32(0.0), north_wind)
    east_below = shifted(east_face[:, -1:, :], "gx", 1)
    north_below = shifted(north_face[:, :, -1:], "gy", 1)
    east_ext = jnp.concatenate([east_below, east_face, jnp.zeros_like(east_below)], axis=1)
    east_ext = jnp.pad(east_ext, ((0, 0), (0, 0), (1, 1)))
    north_ext = jnp.concatenate([north_below, north_face, jnp.zeros_like(north_below)], axis=2)
    north_ext = jnp.pad(north_ext, ((0, 0), (1, 1), (0, 0)))
    wind_ext = jnp.stack([east_ext, north_ext])
    advected = nudged
    for sweep in range(2):
        field_ext = padded(advected, (("gx", 2), ("gy", 3)), 1)
        advected = upwind(field_ext, wind_ext)
    return (advected, coeffs)


def split(value):
    high = value.astype(jnp.bfloat16)
    return high, (value - high.astype(jnp.float32)).astype(jnp.bfloat16)


def split_table(table):
    table = np.asarray(table, np.float32)
    high = table.astype(ml_dtypes.bfloat16)
    low = (table - high.astype(np.float32)).astype(ml_dtypes.bfloat16)
    return high, low


def table64(total, modes):
    index = np.arange(total)[:, None]
    wave = np.arange(modes)[None, :]
    weight = np.where(wave == 0, math.sqrt(1.0 / total), math.sqrt(2.0 / total))
    turns = (wave * (2 * index + 1)) % (4 * total)
    return np.cos(turns * (math.pi / (2.0 * total))) * weight


def dot(a, b):
    return jnp.dot(a, b, preferred_element_type=jnp.float32)


def tables(gxn, gyn, strip, band):
    bx = table64(gxn * strip, MX)
    by = table64(gyn * band, MY)
    half = strip // 2
    forward_y = np.zeros((gyn, 2 * band, 2 * MY))
    for g in range(gyn):
        own = by[g * band : (g + 1) * band]
        forward_y[g, :band, :MY] = own
        forward_y[g, band:, MY:] = own
    wy = np.stack(split_table(forward_y), axis=1)
    bx4 = bx.reshape(gxn, 2, half, MX // 2, 2)
    forward_x = np.broadcast_to(
        bx4.transpose(1, 4, 3, 0, 2)[:, :, :, :, None, :], (2, 2, MX // 2, gxn, gyn, half)
    )
    wx = np.stack(split_table(forward_x.reshape(2 * MX, gxn * gyn * half)))
    inverse_x = np.zeros((gxn, 2, strip + 8, MX // 2))
    for g in range(gxn):
        for row in range(strip + 8):
            if row < strip + 2:
                x = g * strip + row
            elif row >= strip + 6:
                x = g * strip + row - strip - 8
            else:
                continue
            if 0 <= x < gxn * strip:
                inverse_x[g, :, row] = bx[x].reshape(MX // 2, 2).T
    high, low = split_table(inverse_x.reshape(gxn, 2 * (strip + 8), MX // 2))
    xb = np.concatenate([high, high, low], axis=2)
    inverse_y = np.zeros((gyn, 2 * MY, gyn * band))
    for g in range(gyn):
        rolled = 0.5 * np.roll(by, -g * band, axis=0).T
        inverse_y[g, :MY] = rolled
        inverse_y[g, MY:] = rolled
    wi = np.stack(split_table(inverse_y), axis=1)
    return wy, wx, xb, wi


def spectral_kernel(
    field_in, driver_in, east_in, north_in, wy_in, wx_in, xb_in, wi_in, coef_out, advected,
    coef, out, packed, flat, stores, field, driver, east, north, wy, wx, xb, wi,
    part, recv, edge, ysend, wind, halo, ytile, full, winds, large, loads,
    a2a_s, a2a_r, halo_s, halo_r, y_s, y_r, z_s, z_r, p2_s, p2_r, p3_s, p3_r, core_s, core_r,
):
    gx = lax.axis_index("gx")
    gy = lax.axis_index("gy")
    gxn, gyn = lax.axis_size("gx"), lax.axis_size("gy")
    count = gxn * gyn
    me = gx * gyn + gy
    fields, strip, band = field.shape
    levels = east.shape[0]
    own = fields // count
    ext = strip + 8
    total = fields + 2 * levels
    chunk = 4 * own
    chunks = fields // chunk

    def load(src, dst, index):
        return pltpu.make_async_copy(src, dst, loads.at[index])

    def piece(src, dst, c, index):
        rows = pl.ds(c * chunk, chunk)
        return load(src.at[rows], dst.at[rows], index)

    y_table = load(wy_in.at[gy], wy, 0)
    x_table = load(wx_in, wx, 1)
    small = [
        load(east_in, east, 2),
        load(north_in, north, 3),
        load(xb_in.at[gx], xb, 4),
        load(wi_in.at[gy], wi, 5),
    ]
    pieces = [
        (piece(field_in, field, c, 6 + c), piece(driver_in, driver, c, 6 + chunks + c))
        for c in range(chunks)
    ]
    y_table.start()
    for a, b in pieces:
        a.start()
        b.start()
    x_table.start()
    for copy in small:
        copy.start()

    barrier = pltpu.get_barrier_semaphore()

    def greet(rel, carry):
        d = (me + rel) % count
        pl.semaphore_signal(
            barrier, inc=1, device_id=(d // gyn, d % gyn), device_id_type=MESH
        )
        return carry

    lax.fori_loop(1, count, greet, 0)

    y_table.wait()
    wh, wl = wy[0], wy[1]
    for c in range(chunks):
        pieces[c][0].wait()
        pieces[c][1].wait()
        rows = pl.ds(c * chunk, chunk)
        departure = driver[rows] - field[rows]
        lhs = jnp.concatenate([departure[:, : strip // 2], departure[:, strip // 2 :]], axis=2)
        high, low = split(lhs.reshape(chunk * strip // 2, 2 * band))
        got = dot(high, wh) + (dot(low, wh) + dot(high, wl))
        part[pl.ds(c * 4, 4)] = got.reshape(4, own, strip // 2, 2 * MY)
    pl.semaphore_wait(barrier, count - 1)

    def exchange(d, s):
        return pltpu.make_async_remote_copy(
            src_ref=part.at[d], dst_ref=recv.at[s], send_sem=a2a_s.at[d], recv_sem=a2a_r.at[s],
            device_id=(d // gyn, d % gyn), device_id_type=MESH,
        )

    def send(rel, carry):
        exchange((me + rel) % count, me).start()
        return carry

    lax.fori_loop(1, count, send, 0)
    recv[me] = part[me]

    for copy in small:
        copy.wait()
    x_table.wait()
    row = lax.broadcasted_iota(jnp.int32, (levels, strip, band), 1) + gx * strip
    wind[pl.ds(0, levels)] = jnp.where(row == gxn * strip - 1, 0.0, east[...])
    col = lax.broadcasted_iota(jnp.int32, (levels, strip, band), 2) + gy * band
    wind[pl.ds(levels, levels)] = jnp.where(col == gyn * band - 1, 0.0, north[...])

    for side in range(2):
        for k in range(2):
            r = (strip - 2 if side == 0 else 0) + k
            edge[side, k, pl.ds(0, fields)] = field[:, r, :]
            edge[side, k, pl.ds(fields, 2 * levels)] = wind[:, r, :]

    def halo_copy(side, dy):
        peer = gx + 1 if side == 0 else gx - 1
        return pltpu.make_async_remote_copy(
            src_ref=edge.at[side], dst_ref=halo.at[side, dy],
            send_sem=halo_s.at[side, dy], recv_sem=halo_r.at[side, dy],
            device_id=(peer, gy), device_id_type=MESH,
        )

    @pl.when(gx < gxn - 1)
    def _():
        halo_copy(0, 0).start()

    @pl.when(gx > 0)
    def _():
        halo_copy(1, 0).start()

    @pl.when(gx == 0)
    def _():
        halo[0, 0] = jnp.zeros(halo.shape[2:], jnp.float32)

    @pl.when(gx == gxn - 1)
    def _():
        halo[1, 0] = jnp.zeros(halo.shape[2:], jnp.float32)

    for b in range((fields + 2 * levels) // 8):
        if b * 8 < fields:
            block = field[pl.ds(b * 8, 8)]
        else:
            block = wind[pl.ds(b * 8 - fields, 8)]
        turned = block.reshape(8 * strip, band).T
        ysend[b] = jnp.where(gy == 0, turned[band - 8 :], turned[:8])
    ycopy = pltpu.make_async_remote_copy(
        src_ref=ysend, dst_ref=ytile, send_sem=y_s, recv_sem=y_r,
        device_id=(gx, 1 - gy), device_id_type=MESH,
    )

    def receive(rel, carry):
        exchange((me + rel) % count, (me + rel) % count).wait_recv()
        return carry

    lax.fori_loop(1, count, receive, 0)
    rhs = jnp.concatenate(
        [recv[:, j].reshape(count * strip // 2, 2 * MY) for j in range(own)], axis=1
    )
    high, low = split(rhs)
    modes = dot(wx[0], high) + (dot(wx[0], low) + dot(wx[1], high))
    z, y, c, x = gx // 4, (gx // 2) % 2, gx % 2, gy
    hm = MX // 2
    lane = lax.broadcasted_iota(jnp.int32, (hm, 2 * MY), 1)
    for j in range(own):
        q = modes[:, j * 2 * MY : (j + 1) * 2 * MY]
        even = q[:hm] + pltpu.roll(q[2 * hm : 3 * hm], MY, 1)
        odd = pltpu.roll(q[hm : 2 * hm], MY, 1) + q[3 * hm :]
        coef[z, y, c, x, pl.ds(j * hm, hm)] = jnp.where(lane < MY, even, odd)

    part_rows = own * hm // 2
    first, second = pl.ds(0, part_rows), pl.ds(part_rows, part_rows)
    zs = [(z + k) % 4 for k in range(4)]

    def z_copy(k, slot):
        there = coef.at[slot, y, c, x]
        return pltpu.make_async_remote_copy(
            src_ref=there, dst_ref=there, send_sem=z_s.at[k], recv_sem=z_r.at[slot],
            device_id=(zs[k] * 4 + y * 2 + c, gy), device_id_type=MESH,
        )

    def to_x(ref, s, r):
        return pltpu.make_async_remote_copy(
            src_ref=ref, dst_ref=ref, send_sem=s, recv_sem=r,
            device_id=(gx, 1 - gy), device_id_type=MESH,
        )

    def to_y(ref, s, r):
        return pltpu.make_async_remote_copy(
            src_ref=ref, dst_ref=ref, send_sem=s, recv_sem=r,
            device_id=(z * 4 + (1 - y) * 2 + c, gy), device_id_type=MESH,
        )

    def to_core(ref, s, r):
        return pltpu.make_async_remote_copy(
            src_ref=ref, dst_ref=ref, send_sem=s, recv_sem=r,
            device_id=(z * 4 + y * 2 + 1 - c, gy), device_id_type=MESH,
        )

    def second_a(k, xx):
        return to_x(coef.at[zs[k], y, c, xx, first], p2_s.at[0, k], p2_r.at[0, zs[k]])

    def second_b(k, yy):
        return to_y(coef.at[zs[k], yy, c, x, second], p2_s.at[1, k], p2_r.at[1, zs[k]])

    def third_a(k, yy):
        return to_y(coef.at[zs[k], yy, c, :, first], p3_s.at[0, k], p3_r.at[0, zs[k]])

    def third_b(k, xx):
        return to_x(coef.at[zs[k], :, c, xx, second], p3_s.at[1, k], p3_r.at[1, zs[k]])

    def core_copy(k, cc):
        return to_core(coef.at[zs[k], :, cc], core_s.at[k], core_r.at[zs[k]])

    for k in range(1, 4):
        z_copy(k, z).start()
    second_a(0, x).start()
    second_b(0, y).start()

    @pl.when(gx < gxn - 1)
    def _():
        halo_copy(0, 0).wait_send()
        halo_copy(1, 0).wait_recv()

    @pl.when(gx > 0)
    def _():
        halo_copy(1, 0).wait_send()
        halo_copy(0, 0).wait_recv()

    blocks_y = total // 8
    for h in range(2):
        for k in range(2):
            turned = halo[h, 0, k].T
            ysend[blocks_y + 2 * h + k] = jnp.where(gy == 0, turned[band - 8 :], turned[:8])
    ycopy.start()

    for f in range(fields):
        full[0, pl.ds(f * ext, strip)] = field[f]
    for f in range(2 * levels):
        full[0, pl.ds((fields + f) * ext, strip)] = wind[f]
    blank = jnp.zeros((total, band), jnp.float32)
    for k in range(2):
        full[0, pl.ds(strip + k, total, stride=ext), :] = halo[1, 0, k]
        full[0, pl.ds(strip + 6 + k, total, stride=ext), :] = halo[0, 0, k]
    for d in range(2):
        for k in range(2, 6):
            full[d, pl.ds(strip + k, total, stride=ext), :] = blank
    gap = jnp.zeros((band - 16, 8 * strip), jnp.float32)

    def turn(b):
        tile = ytile[b]
        return jnp.concatenate(
            [jnp.where(gy == 0, tile, 0.0), gap, jnp.where(gy == 1, tile, 0.0)], axis=0
        ).T

    def assemble():
        ycopy.wait()
        for b in range(blocks_y):
            turned = turn(b)
            for i in range(8):
                full[1, pl.ds((b * 8 + i) * ext, strip)] = turned[i * strip : (i + 1) * strip]
        for k in range(2):
            full[1, pl.ds(strip + k, total, stride=ext), :] = turn(blocks_y + 2 + k)
            full[1, pl.ds(strip + 6 + k, total, stride=ext), :] = turn(blocks_y + k)
        for lev in range(levels):
            u, v = extended(fields + lev), extended(fields + levels + lev)
            winds[lev, 0] = jnp.maximum(u, 0.0)
            winds[lev, 1] = jnp.minimum(u, 0.0)
            winds[lev, 2] = jnp.maximum(v, 0.0)
            winds[lev, 3] = jnp.minimum(v, 0.0)

    def extended(f):
        rows = pl.ds(pl.multiple_of(f * ext, 8), ext)
        return jnp.concatenate([full[0, rows], full[1, rows]], axis=1)

    lane = lax.broadcasted_iota(jnp.int32, (ext, 2 * MY), 1)

    def store(src, dst, slot, index):
        rows = pl.ds(pl.multiple_of(slot * (fields // 4), 8), fields // 4)
        return pltpu.make_async_copy(src.at[rows], dst.at[rows], stores.at[index, slot])

    def compute(slot):
        base = slot * (fields // 4)

        def inverse(i, carry):
            rows = coef.at[slot, i // 4, (i // 2) % 2, i % 2]
            blocks = [rows[pl.ds(j * hm, hm)] for j in range(own)]
            for j in range(own):
                flat[pl.ds(pl.multiple_of((i * own + j) * hm, hm), hm)] = blocks[j]
            joined = jnp.concatenate(blocks, axis=1)
            high, low = split(joined)
            mixed = dot(xb[...], jnp.concatenate([high, low, high], axis=0))
            stack = []
            for j in range(own):
                one = mixed[:, j * 2 * MY : (j + 1) * 2 * MY]
                stack.append(jnp.where(lane < MY, one[:ext], one[ext:]))
            high, low = split(jnp.concatenate(stack, axis=0))
            got = dot(high, wi[0]) + (dot(low, wi[0]) + dot(high, wi[1]))
            large[pl.ds(i * own, own)] = got.reshape(own, ext, gyn * band)
            return carry

        lax.fori_loop(0, fields // own // 4, inverse, 0, unroll=8)
        held = pl.ds(pl.multiple_of(base, 8), fields // 4)
        for j in range(hm):
            packed[held, pl.ds(j * 2 * MY, 2 * MY)] = flat[pl.ds(j, fields // 4, stride=hm), :]
        store(packed, coef_out, slot, 1).start()

        def tracer(i, carry):
            f = base + i
            lev = f % levels
            up, un, vp, vn = winds[lev, 0], winds[lev, 1], winds[lev, 2], winds[lev, 3]
            q = extended(f) + large[i]
            for _ in range(2):
                flux = up * q + un * pltpu.roll(q, ext - 1, 0)
                cross = vp * q + vn * pltpu.roll(q, gyn * band - 1, 1)
                q = q - (flux - pltpu.roll(flux, 1, 0))
                q = q - (cross - pltpu.roll(cross, 1, 1))
            out[f] = q[:strip, :band]
            return carry

        lax.fori_loop(0, fields // 4, tracer, 0, unroll=12)
        store(out, advected, slot, 0).start()

    for step in range(1, 7):
        if step < 4:
            z_copy(step, zs[step]).wait_recv()
            second_a(step, x).start()
            second_b(step, y).start()
        k = step - 1
        if k < 4:
            second_a(k, 1 - x).wait_recv()
            second_b(k, 1 - y).wait_recv()
            third_a(k, y).start()
            third_b(k, x).start()
        k = step - 2
        if 0 <= k < 4:
            third_a(k, 1 - y).wait_recv()
            third_b(k, 1 - x).wait_recv()
            core_copy(k, c).start()
        if step == 2:
            assemble()
        k = step - 3
        if k >= 0:
            core_copy(k, 1 - c).wait_recv()
            compute(zs[k])

    for k in range(1, 4):
        z_copy(k, z).wait_send()
    for k in range(4):
        second_a(k, x).wait_send()
        second_b(k, y).wait_send()
        third_a(k, y).wait_send()
        third_b(k, x).wait_send()
        core_copy(k, c).wait_send()

    def drain(rel, carry):
        exchange((me + rel) % count, me).wait_send()
        return carry

    lax.fori_loop(1, count, drain, 0)
    for k in range(4):
        store(out, advected, zs[k], 0).wait()
        store(packed, coef_out, zs[k], 1).wait()


def write_kernel(coef, advected, coef_out, advected_out, coef_v, advected_v, ins, outs):
    inward, outward = [], []
    arrays = ((coef, coef_v, coef_out), (advected, advected_v, advected_out))
    for i, (src, mid, dst) in enumerate(arrays):
        rows = src.shape[0] // 4
        for k in range(4):
            part = pl.ds(k * rows, rows)
            inward.append(pltpu.make_async_copy(src.at[part], mid.at[part], ins.at[i, k]))
            outward.append(pltpu.make_async_copy(mid.at[part], dst.at[part], outs.at[i, k]))
    for copy in inward:
        copy.start()
    for a, b in zip(inward, outward):
        a.wait()
        b.start()
    for copy in outward:
        copy.wait()


def fused(field, driver, east, north):
    tracers, levels, strip, band = field.shape
    gxn, gyn = lax.axis_size("gx"), lax.axis_size("gy")
    count = gxn * gyn
    fields = tracers * levels
    own = fields // count
    total = fields + 2 * levels
    wy, wx, xb, wi = tables(gxn, gyn, strip, band)
    flat = field.reshape(fields, strip, band)
    dma = pltpu.SemaphoreType.DMA
    f32 = jnp.float32
    bf16 = jnp.bfloat16
    hbm = pl.BlockSpec(memory_space=pltpu.HBM)
    coeffs, advected = pl.pallas_call(
        spectral_kernel,
        out_shape=(
            jax.ShapeDtypeStruct((fields, MX * MY), f32),
            jax.ShapeDtypeStruct((fields, strip, band), f32),
        ),
        in_specs=[hbm] * 8,
        out_specs=(hbm, hbm),
        scratch_shapes=[
            pltpu.VMEM((4, 2, 2, 2, own * MX // 2, 2 * MY), f32),
            pltpu.VMEM((fields, strip, band), f32),
            pltpu.VMEM((fields, MX * MY), f32),
            pltpu.VMEM((fields // 4 * MX // 2, 2 * MY), f32),
            dma((2, 4)),
            pltpu.VMEM((fields, strip, band), f32),
            pltpu.VMEM((fields, strip, band), f32),
            pltpu.VMEM((levels, strip, band), f32),
            pltpu.VMEM((levels, strip, band), f32),
            pltpu.VMEM(wy.shape[1:], bf16),
            pltpu.VMEM(wx.shape, bf16),
            pltpu.VMEM(xb.shape[1:], bf16),
            pltpu.VMEM(wi.shape[1:], bf16),
            pltpu.VMEM((count, own, strip // 2, 2 * MY), f32),
            pltpu.VMEM((count, own, strip // 2, 2 * MY), f32),
            pltpu.VMEM((2, 2, total, band), f32),
            pltpu.VMEM((total // 8 + 4, 8, 8 * strip), f32),
            pltpu.VMEM((2 * levels, strip, band), f32),
            pltpu.VMEM((2, 1, 2, total, band), f32),
            pltpu.VMEM((total // 8 + 4, 8, 8 * strip), f32),
            pltpu.VMEM((gyn, total * (strip + 8), band), f32),
            pltpu.VMEM((levels, 4, strip + 8, gyn * band), f32),
            pltpu.VMEM((fields // 4, strip + 8, gyn * band), f32),
            dma((6 + 2 * (fields // (4 * own)),)),
            dma((count,)), dma((count,)), dma((2, 1)), dma((2, 1)), dma, dma,
            dma((4,)), dma((4,)), dma((2, 4)), dma((2, 4)), dma((2, 4)), dma((2, 4)),
            dma((4,)), dma((4,)),
        ],
        compiler_params=pltpu.CompilerParams(
            collective_id=0, has_side_effects=True, vmem_limit_bytes=62 << 20
        ),
        name="spectral",
    )(
        flat, driver.reshape(fields, strip, band), east, north,
        jnp.asarray(wy), jnp.asarray(wx), jnp.asarray(xb), jnp.asarray(wi),
    )
    coeffs, advected = pl.pallas_call(
        write_kernel,
        out_shape=(
            jax.ShapeDtypeStruct((fields, MX * MY), f32),
            jax.ShapeDtypeStruct((fields, strip, band), f32),
        ),
        in_specs=[hbm] * 2,
        out_specs=(hbm, hbm),
        scratch_shapes=[
            pltpu.VMEM((fields, MX * MY), f32),
            pltpu.VMEM((fields, strip, band), f32),
            dma((2, 4)),
            dma((2, 4)),
        ],
        compiler_params=pltpu.CompilerParams(vmem_limit_bytes=62 << 20),
        name="write",
    )(coeffs, advected)
    return (
        advected.reshape(tracers, levels, strip, band),
        coeffs.reshape(tracers, levels, MX * MY),
    )


def body(field, driver, east, north):
    tracers, levels, strip, band = field.shape
    sizes = (lax.axis_size("gx"), lax.axis_size("gy"))
    if sizes == (16, 2) and (tracers * levels, levels, strip, band) == (96, 16, 16, 128):
        return fused(field, driver, east, north)
    return shards(field, driver, east, north)


def solution(mesh):
    placed = (
        P(None, None, "gx", "gy"),
        P(None, None, "gx", "gy"),
        P(None, "gx", "gy"),
        P(None, "gx", "gy"),
    )
    return jax.shard_map(
        body,
        mesh=mesh,
        in_specs=placed,
        out_specs=(P(None, None, "gx", "gy"), P()),
        check_vma=False,
    )
```
